256 devices in a mesh: grp: 16 (over z, core), mem: 16 (over y, x).
Axes of the slice: x: 4, y: 4, z: 8, core: 2. Of those that a mesh axis runs over, the one named last changes fastest.
Arguments:
- background: bfloat16 [256, 1024, 512], P('mem', 'grp'), may hold values from -6 to 6
- obs_pert: bfloat16 [1024, 2048, 256], P(('grp', 'mem')), may hold values from -24 to 24
- obs_innov: bfloat16 [1024, 2048], P(('grp', 'mem')), may hold values from -6 to 6
- obs_rinv: bfloat16 [1024, 2048], P(('grp', 'mem')), may hold values from 0.25 to 2.5
- obs_pos: bfloat16 [1024, 2048], P(('grp', 'mem')), may hold values from 0 to 1
- obs_count: int32 [1024], P(('grp', 'mem')), may hold values from 1 to 2048, as said below
Outputs:
- analysis: bfloat16 [256, 1024, 512], P('mem', 'grp')
The draws below stay inside these ranges and needn't reach their ends.
Inputs may be any that keep to these rules, and one draw needn't show every extreme that they name: The observations of patch p sit in its first obs_count[p] slots; the slots after them hold no observation.
All inputs are finite; a program needn't handle non-finite values.
Results may differ from the reference program's by a relative error of at most 0.0058.
Values may be sent and summed in bfloat16 or wider, within the bound.
No kernel may reach another device: no remote copies, remote signals or barrier semaphores. Data moves between devices by JAX's collectives and lax.ppermute only.
A program may use at most 64 MiB of HBM per device.

```python
import math
import jax
import jax.numpy as jnp
from jax import lax

K = 256
P_SIZE = 512
PAT_DEV = 4
SLOTS = 2048
BLOCK = 128
NS_STEPS = 8
PATCHES = 1024
N_GRP = 16
N_MEM = 16


def draw_obs_pert(key, part):
    first_key, second_key = jax.random.split(jax.random.fold_in(key, 11), 2)
    base = jax.random.normal(first_key, (PATCHES, SLOTS, K), jnp.float32)
    row_scale = jnp.exp(jax.random.uniform(second_key, (PATCHES, SLOTS, 1), jnp.float32, math.log(0.4), math.log(1.2)))
    values = row_scale * base
    return jnp.clip(values, -24.0, 24.0).astype(jnp.bfloat16)


def draw_obs_count(key, part):
    level_key, blocks_key, heavy_key, tail_key = jax.random.split(jax.random.fold_in(key, 23), 4)
    blocks_all = SLOTS // BLOCK
    device_total = PATCHES // PAT_DEV
    level = jax.random.randint(level_key, (device_total,), 0, 3)
    reach = jnp.maximum(1, blocks_all // 4 * (1 + level))
    reach = jnp.repeat(reach, PAT_DEV)
    raw_value = jax.random.randint(blocks_key, (PATCHES,), 0, 1 << 20)
    blocks = 1 + raw_value % reach
    heavy = jax.random.randint(heavy_key, (), 0, device_total)
    partner = (heavy // N_MEM + N_GRP // 2) % N_GRP * N_MEM + heavy % N_MEM
    owner = jnp.arange(PATCHES) // PAT_DEV
    blocks = jnp.where(owner == partner, 1, blocks)
    tail_count = jax.random.randint(tail_key, (PATCHES,), 1, BLOCK + 1)
    counted = (blocks - 1) * BLOCK + tail_count
    return jnp.where(owner == heavy, SLOTS, counted).astype(jnp.int32)


def levels(stream_key, extent, shards, low, high):
    factor_of, own = 1.0, jax.random.fold_in(stream_key, 6)
    for dim, blocks in shards:
        heights = jnp.exp(jax.random.uniform(jax.random.fold_in(own, dim), (blocks,), jnp.float32, low / len(shards), high / len(shards)))
        factor_of = factor_of * jnp.repeat(heights, extent[dim] // blocks).reshape([-1 if axis == dim else 1 for axis in range(len(extent))])
    return factor_of


def scatter_about(rng, extent, scale, bound, cuts=(), kind=jnp.bfloat16):
    entries = jax.random.normal(rng, extent, jnp.float32) * scale
    if len(cuts) > 0:
        entries = levels(rng, extent, cuts, -0.22, 0.18) * entries
    return jnp.clip(entries, min=-bound, max=bound).astype(kind)


def setup_inputs(seed: int = 0) -> dict:
    splits = jax.random.split(jax.random.key(seed), 7)
    return {
        "background": scatter_about(splits[0], (K, PATCHES, P_SIZE), 1.0, 6.0, ((0, 16), (1, 16))),
        "obs_pert": draw_obs_pert(jax.random.fold_in(splits[6], 71), 0),
        "obs_innov": scatter_about(splits[2], (PATCHES, SLOTS), 1.0, 6.0, ((0, 256),)),
        "obs_rinv": jnp.clip(jnp.exp(math.log(2.5) - 2.3025851 * jax.random.uniform(splits[3], (PATCHES, SLOTS), jnp.float32) ** levels(splits[3], (PATCHES, SLOTS), ((0, 256),), -0.2, 0.2)), 0.25, 2.5).astype(jnp.bfloat16),
        "obs_pos": jnp.clip(1.0 * jax.random.uniform(splits[4], (PATCHES, SLOTS), jnp.float32) ** levels(splits[4], (PATCHES, SLOTS), ((0, 256),), -0.2, 0.2), 0.0, 1.0).astype(jnp.bfloat16),
        "obs_count": draw_obs_count(jax.random.fold_in(splits[6], 71), 0),
    }


LOC_SCALE = 0.8

def locality(position, inv_var, offset):
    distance = position - 0.5 - offset
    return inv_var * jnp.exp(-distance * distance / (2.0 * LOC_SCALE * LOC_SCALE))

def root_inverse(matrix):
    members = matrix.shape[-1]
    identity = jnp.eye(members, dtype=jnp.float32)
    total = jnp.trace(matrix, axis1=-2, axis2=-1)
    current = matrix / total[..., None, None]
    inverse = jnp.broadcast_to(identity, matrix.shape)
    for step_number in range(NS_STEPS):
        middle = 1.5 * identity - 0.5 * jnp.matmul(inverse, current, precision=lax.Precision.HIGHEST)
        current = jnp.matmul(current, middle, precision=lax.Precision.HIGHEST)
        inverse = jnp.matmul(middle, inverse, precision=lax.Precision.HIGHEST)
    return (inverse, total)

def reference(background, obs_pert, obs_innov, obs_rinv, obs_pos, obs_count):
    slot_index = jnp.arange(SLOTS, dtype=jnp.int32)
    identity = jnp.eye(K, dtype=jnp.float32)

    def one_patch(target):
        gram_sum = jnp.zeros((K, K), jnp.float32)
        vec_sum = jnp.zeros((K,), jnp.float32)
        for offset in (-1, 0, 1):
            source = ((target - offset) % PATCHES).astype(jnp.int32)
            obs_rows = lax.dynamic_index_in_dim(obs_pert, source, 0, keepdims=False)
            position = lax.dynamic_index_in_dim(obs_pos, source, 0, keepdims=False).astype(jnp.float32)
            inv_var = lax.dynamic_index_in_dim(obs_rinv, source, 0, keepdims=False).astype(jnp.float32)
            departure = lax.dynamic_index_in_dim(obs_innov, source, 0, keepdims=False).astype(jnp.float32)
            count_here = lax.dynamic_index_in_dim(obs_count, source, 0, keepdims=False)
            live = slot_index < count_here
            weight = jnp.where(live, locality(position, inv_var, offset), jnp.float32(0.0))
            widened = obs_rows.astype(jnp.float32)
            scaled = (widened * weight[:, None]).astype(jnp.bfloat16)
            gram_sum = gram_sum + jnp.dot(scaled.T, obs_rows, preferred_element_type=jnp.float32)
            vec_sum = vec_sum + jnp.dot(weight * departure, widened, precision=lax.Precision.HIGHEST)
        matrix = gram_sum + (K - 1.0) * identity
        inverse, total = root_inverse(matrix)
        covariance = jnp.matmul(inverse, inverse, precision=lax.Precision.HIGHEST) / total
        mean_weights = jnp.dot(covariance, vec_sum, precision=lax.Precision.HIGHEST)
        transform = (jnp.sqrt((K - 1.0) / total) * inverse + mean_weights[:, None]).astype(jnp.bfloat16)
        state = lax.dynamic_index_in_dim(background, target, 1, keepdims=False).astype(jnp.float32)
        center = lax.optimization_barrier(jnp.mean(state, axis=0))
        spread = (state - center[None, :]).astype(jnp.bfloat16)
        result = jnp.dot(transform.T, spread, preferred_element_type=jnp.float32) + center[None, :]
        return result.astype(jnp.bfloat16)
    stacked = lax.map(one_patch, jnp.arange(PATCHES, dtype=jnp.int32))
    return jnp.transpose(stacked, (1, 0, 2))
```

```python
import functools
import jax
import jax.numpy as jnp
from jax import lax
from jax.experimental import pallas as pl
from jax.experimental.pallas import tpu as pltpu
from jax.sharding import PartitionSpec as P

NS_STEPS = 8
LOC_SCALE = 0.8
CHUNK = 1024
OFFSETS = (-1, 0, 1)
RING = ("grp", "mem")
VROWS = 8
F32 = jnp.float32
BF16 = jnp.bfloat16


def locality(position, inv_var, offset):
    distance = position - 0.5 - offset
    return inv_var * jnp.exp(-distance * distance / (2.0 * LOC_SCALE * LOC_SCALE))


def chunk_products(place, patch, start, counts, obs, innov, rinv, pos, rows_buf, lhs, acc, accv):
    members = obs.shape[-1]
    depth = rows_buf.shape[1]
    count = counts[patch]
    slot = start + lax.broadcasted_iota(jnp.int32, (1, depth), 1)
    live = slot < count
    lanes = pl.ds(pl.multiple_of(start, depth), depth)
    position = pos[pl.ds(patch, 1), lanes]
    inv_var = jnp.where(live, rinv[pl.ds(patch, 1), lanes], 0.0)
    departure = innov[pl.ds(patch, 1), lanes]
    turned = rows_buf[place].T.astype(F32)
    row = lax.broadcasted_iota(jnp.int32, (4 * VROWS, depth), 0)
    vec_rows = jnp.zeros((4 * VROWS, depth), F32)
    for number, offset in enumerate(OFFSETS):
        weight = locality(position, inv_var, offset)
        lhs[number * members : (number + 1) * members, :] = (turned * weight).astype(BF16)
        moved = weight * departure
        high = moved.astype(BF16).astype(F32)
        vec_rows = jnp.where(row == number * VROWS, high, vec_rows)
        vec_rows = jnp.where(row == number * VROWS + 1, moved - high, vec_rows)
    lhs[3 * members :, :] = vec_rows.astype(BF16)
    product = jnp.dot(lhs[...], rows_buf[place], preferred_element_type=F32)
    first = pl.ds(pl.multiple_of(patch * members, members), 3 * members)
    acc[first, :] += product[: 3 * members]
    first_v = pl.ds(pl.multiple_of(patch * VROWS, VROWS), 3 * VROWS)
    accv[first_v, :] += product[3 * members : 3 * members + 3 * VROWS]


def gram_loop(patches, counts, obs, innov, rinv, pos, rows_buf, sems, lhs, acc, accv):
    depth = rows_buf.shape[1]
    per_patch = obs.shape[1] // depth

    def copy_of(place, patch, start):
        rows = pl.ds(pl.multiple_of(start, depth), depth)
        return pltpu.make_async_copy(obs.at[patch, rows], rows_buf.at[place], sems.at[place])

    first, step = patches[0], patches[1] - patches[0]

    def where_is(place):
        return first + place // per_patch * step, place % per_patch * depth

    for place in range(2 * per_patch):
        patch, start = where_is(place)

        @pl.when(start < counts[patch])
        def _():
            copy_of(place, patch, start).start()

    def body(place, carry):
        patch, start = where_is(place)

        @pl.when(start < counts[patch])
        def _():
            copy_of(place, patch, start).wait()
            chunk_products(
                place, patch, start, counts, obs, innov, rinv, pos, rows_buf, lhs, acc, accv
            )

        return carry

    return lambda: lax.fori_loop(0, 2 * per_patch, body, 0)


def edge_kernel(counts, obs, innov, rinv, pos, send, kept, kept_v, rows_buf, sems, lhs, acc, accv):
    members = obs.shape[-1]
    last = obs.shape[0] - 1
    run = gram_loop((0, last), counts, obs, innov, rinv, pos, rows_buf, sems, lhs, acc, accv)
    acc[...] = jnp.zeros_like(acc)
    accv[...] = jnp.zeros_like(accv)
    run()
    kept[...] = acc[members:-members, :]
    kept_v[...] = accv[VROWS:-VROWS, :]
    row = lax.broadcasted_iota(jnp.int32, (2 * VROWS, members), 0)
    for side, slot in enumerate((0, last + 2)):
        send[side, :members, :] = acc[slot * members : (slot + 1) * members, :].astype(BF16)
        total = (
            accv[slot * VROWS : slot * VROWS + 1, :] + accv[slot * VROWS + 1 : slot * VROWS + 2, :]
        )
        high = total.astype(BF16).astype(F32)
        tail = jnp.where(row == 0, high, jnp.where(row == 1, total - high, 0.0))
        send[side, members:, :] = tail.astype(BF16)


def inner_kernel(
    counts, obs, innov, rinv, pos, kept, kept_v, out, out_v, rows_buf, sems, lhs, acc, accv
):
    members = obs.shape[-1]
    run = gram_loop((1, 2), counts, obs, innov, rinv, pos, rows_buf, sems, lhs, acc, accv)
    acc[members:-members, :] = kept[...]
    accv[VROWS:-VROWS, :] = kept_v[...]
    run()
    out[...] = acc[members:-members, :]
    out_v[...] = accv[VROWS:-VROWS, :]


def gram_call(kernel, name, extra, outs, counts, obs, innov, rinv, pos):
    patches, slots, members = obs.shape
    vmem = pl.BlockSpec(memory_space=pltpu.VMEM)
    pieces = 2 * (slots // CHUNK)
    return pl.pallas_call(
        kernel,
        name=name,
        out_shape=outs,
        in_specs=[
            pl.BlockSpec(memory_space=pltpu.SMEM),
            pl.BlockSpec(memory_space=pl.ANY),
            vmem,
            vmem,
            vmem,
        ]
        + [vmem] * len(extra),
        out_specs=[vmem] * len(outs),
        scratch_shapes=[
            pltpu.VMEM((pieces, CHUNK, members), BF16),
            pltpu.SemaphoreType.DMA((pieces,)),
            pltpu.VMEM((3 * members + 4 * VROWS, CHUNK), BF16),
            pltpu.VMEM(((patches + 2) * members, members), F32),
            pltpu.VMEM(((patches + 2) * VROWS, members), F32),
        ],
        compiler_params=pltpu.CompilerParams(vmem_limit_bytes=32 << 20),
        cost_estimate=pl.CostEstimate(
            flops=6 * 2 * slots * members * members,
            bytes_accessed=2 * slots * members * 2,
            transcendentals=6 * slots,
        ),
    )(counts, obs, innov, rinv, pos, *extra)


def scalar_steps():
    return (2.25, -2.4375, 1.6875, -0.5625, 0.0625)


def root_kernel(gram, gram_v, from_before, from_after, transform, y_dev, z_dev, p_dev, s_dev):
    members = gram.shape[1]
    patches = gram.shape[0] // members
    row = lax.broadcasted_iota(jnp.int32, (members, members), 0)
    col = lax.broadcasted_iota(jnp.int32, (members, members), 1)
    diagonal = row == col

    def times(a, a_s, b, b_s):
        product = jnp.dot(a.astype(BF16), b.astype(BF16), preferred_element_type=F32)
        return product + a_s * b + b_s * a, a_s * b_s

    totals, vecs = [], []
    for t in range(patches):
        here = gram[t * members : (t + 1) * members, :]
        vec = gram_v[t * VROWS : t * VROWS + 1, :] + gram_v[t * VROWS + 1 : t * VROWS + 2, :]
        for side, edge in ((from_before, 0), (from_after, patches - 1)):
            if t == edge:
                here = here + side[:members, :].astype(F32)
                tail = side[members:, :].astype(F32)
                vec = vec + tail[0:1, :] + tail[1:2, :]
        trace = jnp.sum(jnp.where(diagonal, here, 0.0)) + members * (members - 1.0)
        scale = 1.0 / trace
        y_dev[t] = here * scale + jnp.where(diagonal, (members - 1.0) * scale - 1.0 / members, 0.0)
        totals.append(trace)
        vecs.append(vec)
    a0, a1, a2, a3, a4 = scalar_steps()
    y_s, z_s = 1.0 / members, 1.0
    for pair in range(NS_STEPS // 2):
        first, final = pair == 0, pair == NS_STEPS // 2 - 1
        p_s = y_s * z_s
        p2_s = p_s * p_s
        h_s = a2 + a3 * p_s + a4 * p2_s
        q_s = p2_s * h_s + a0 + a1 * p_s
        for t in range(patches):
            p = y_dev[t] if first else times(z_dev[t], z_s, y_dev[t], y_s)[0]
            p_dev[t] = p
        for t in range(patches):
            p = p_dev[t]
            s_dev[t] = times(p, p_s, p, p_s)[0]
        for t in range(patches):
            p, p2 = p_dev[t], s_dev[t]
            s_dev[t] = times(p2, p2_s, a3 * p + a4 * p2, h_s)[0] + a1 * p
        for t in range(patches):
            q = s_dev[t]
            if not final:
                y_dev[t] = times(y_dev[t], y_s, q, q_s)[0]
            z_dev[t] = q if first else times(z_dev[t], z_s, q, q_s)[0]
        y_s, z_s = y_s * q_s, z_s * q_s
    for t in range(patches):
        z = z_dev[t] + jnp.where(diagonal, z_s, 0.0)
        once = jnp.sum(z * vecs[t], axis=1, keepdims=True)
        twice = jnp.sum(z * once, axis=0, keepdims=True)
        scale = lax.rsqrt(jnp.full((1, members), totals[t], F32) / (members - 1.0))
        mean_row = twice / totals[t]
        transform[t] = (z * scale + mean_row).astype(BF16)


def root_call(gram, gram_v, from_before, from_after):
    members = gram.shape[1]
    patches = gram.shape[0] // members
    dev = pltpu.VMEM((patches, members, members), F32)
    return pl.pallas_call(
        root_kernel,
        name="root",
        out_shape=jax.ShapeDtypeStruct((patches, members, members), BF16),
        scratch_shapes=[dev] * 4,
        compiler_params=pltpu.CompilerParams(vmem_limit_bytes=32 << 20),
        cost_estimate=pl.CostEstimate(
            flops=17 * patches * 2 * members**3, bytes_accessed=2 << 20, transcendentals=0
        ),
    )(gram, gram_v, from_before, from_after)


def apply_kernel(transform, state, out):
    shares, patches, local, width = state.shape
    members = shares * local
    for t in range(patches):
        wide = state[:, t].reshape(members, width).astype(F32)
        center = jnp.sum(wide, axis=0, keepdims=True) * (1.0 / members)
        spread = (wide - center).astype(BF16)
        result = jnp.dot(transform[t], spread, preferred_element_type=F32) + center
        out[:, t] = result.astype(BF16).reshape(shares, local, width)


def apply_call(transform, state):
    patches, members, _ = transform.shape
    return pl.pallas_call(
        apply_kernel,
        name="apply",
        out_shape=jax.ShapeDtypeStruct(state.shape, BF16),
        compiler_params=pltpu.CompilerParams(vmem_limit_bytes=32 << 20),
        cost_estimate=pl.CostEstimate(
            flops=2 * members * state.size, bytes_accessed=4 * state.size, transcendentals=0
        ),
    )(transform, state)


def on_device(background, obs_pert, obs_innov, obs_rinv, obs_pos, obs_count):
    patches, slots, members = obs_pert.shape
    local, group_patches, width = background.shape
    shares = members // local
    by_patch = jnp.swapaxes(background, 0, 1)
    state = lax.all_to_all(by_patch, "mem", split_axis=0, concat_axis=0, tiled=True)
    state = state.reshape(shares, patches, local, width)

    innov, rinv, pos = (a.astype(F32) for a in (obs_innov, obs_rinv, obs_pos))
    sums = [
        jax.ShapeDtypeStruct((patches * members, members), F32),
        jax.ShapeDtypeStruct((patches * VROWS, members), F32),
    ]
    edge = [jax.ShapeDtypeStruct((2, members + 2 * VROWS, members), BF16)]
    send, kept, kept_v = gram_call(
        edge_kernel, "edge", (), edge + sums, obs_count, obs_pert, innov, rinv, pos
    )
    size = lax.axis_size(RING)
    up = [(i, (i + 1) % size) for i in range(size)]
    down = [(j, i) for i, j in up]
    from_after = lax.ppermute(send[0], RING, down)
    from_before = lax.ppermute(send[1], RING, up)
    gram, gram_v = gram_call(
        inner_kernel, "inner", (kept, kept_v), sums, obs_count, obs_pert, innov, rinv, pos
    )
    transform = root_call(gram, gram_v, from_before, from_after)
    result = apply_call(transform, state)
    result = result.reshape(group_patches, local, width)
    result = lax.all_to_all(result, "mem", split_axis=0, concat_axis=0, tiled=True)
    return jnp.swapaxes(result, 0, 1)


def solution(mesh):
    return jax.shard_map(
        on_device,
        mesh=mesh,
        in_specs=(
            P("mem", "grp", None),
            P(("grp", "mem"), None, None),
            P(("grp", "mem"), None),
            P(("grp", "mem"), None),
            P(("grp", "mem"), None),
            P(("grp", "mem")),
        ),
        out_specs=P("mem", "grp", None),
        check_vma=False,
    )
```

```python
import jax
import jax.numpy as jnp
from jax import lax
from jax.experimental import pallas as pl
from jax.experimental.pallas import tpu as pltpu
from jax.sharding import PartitionSpec as P

NS_STEPS = 8
LOC_SCALE = 0.8
CHUNK = 1024
OFFSETS = (-1, 0, 1)
RING = ("grp", "mem")
VROWS = 8
LANES = 128
MOST_VMEM = 40 << 20
F32 = jnp.float32
BF16 = jnp.bfloat16


def in_hbm(array):
    return pltpu.with_memory_space_constraint(array, pltpu.HBM)


def locality(position, inv_var, offset):
    distance = position - 0.5 - offset
    return inv_var * jnp.exp(-distance * distance / (2.0 * LOC_SCALE * LOC_SCALE))


def chunk_products(place, patch, start, offsets, slot, counts, fields, rows_buf, lhs, acc, accv):
    depth, members = rows_buf.shape[1:]
    span = len(offsets)
    live = start + lax.broadcasted_iota(jnp.int32, (1, depth), 1) < counts[patch]
    lanes = pl.ds(pl.multiple_of(start, depth), depth)
    position = fields[2, pl.ds(patch, 1), lanes]
    inv_var = jnp.where(live, fields[1, pl.ds(patch, 1), lanes], 0.0)
    departure = fields[0, pl.ds(patch, 1), lanes]
    turned = rows_buf[place].T.astype(F32)
    row = lax.broadcasted_iota(jnp.int32, (4 * VROWS, depth), 0)
    vec_rows = jnp.zeros((4 * VROWS, depth), F32)
    for number, offset in enumerate(offsets):
        weight = locality(position, inv_var, offset)
        lhs[number * members : (number + 1) * members, :] = (turned * weight).astype(BF16)
        moved = weight * departure
        high = moved.astype(BF16).astype(F32)
        vec_rows = jnp.where(row == number * VROWS, high, vec_rows)
        vec_rows = jnp.where(row == number * VROWS + 1, moved - high, vec_rows)
    lhs[span * members : span * members + 4 * VROWS, :] = vec_rows.astype(BF16)
    product = jnp.dot(
        lhs[: span * members + 4 * VROWS, :], rows_buf[place], preferred_element_type=F32
    )
    first = pl.ds(pl.multiple_of(slot * members, members), span * members)
    acc[first, :] += product[: span * members]
    first_v = pl.ds(pl.multiple_of(slot * VROWS, VROWS), span * VROWS)
    accv[first_v, :] += product[span * members : span * members + span * VROWS]


def start_rows(pairs, given_counts, counts, count_sem, obs, rows_buf, sems):
    depth = rows_buf.shape[1]
    per_patch = obs.shape[1] // depth
    order = []
    for first, step, base in pairs:
        for place in range(2 * per_patch):
            patch, start = first + place // per_patch * step, place % per_patch * depth
            order.append((patch, start, base + place))

    def begin(patch, start, place):
        pltpu.make_async_copy(
            obs.at[patch, pl.ds(start, depth)], rows_buf.at[place], sems.at[place]
        ).start()

    fetch = pltpu.make_async_copy(given_counts, counts, count_sem)
    fetch.start()
    for patch, start, place in order:
        if start == 0:
            begin(patch, start, place)
    fetch.wait()
    for patch, start, place in order:
        if start > 0:
            pl.when(start < counts[patch])(lambda a=(patch, start, place): begin(*a))


def add_rows(first, step, base, offsets_of, slot_of, counts, obs, fields, bufs):
    rows_buf, sems, lhs, acc, accv = bufs
    depth = rows_buf.shape[1]
    per_patch = obs.shape[1] // depth

    def body(place, carry):
        which = place // per_patch
        patch, start = first + which * step, place % per_patch * depth

        @pl.when(start < counts[patch])
        def _():
            rows = pl.ds(pl.multiple_of(start, depth), depth)
            pltpu.make_async_copy(
                obs.at[patch, rows], rows_buf.at[base + place], sems.at[base + place]
            ).wait()
            chunk_products(
                base + place,
                patch,
                start,
                offsets_of(which),
                slot_of(which),
                counts,
                fields,
                rows_buf,
                lhs,
                acc,
                accv,
            )

        return carry

    lax.fori_loop(0, 2 * per_patch, body, 0)


def by_patch_kernel(
    back, innov, rinv, pos, turned, fields, rows_in, rows_out, narrow, in_sems, out_sems, sems
):
    step = rows_in.shape[2]
    pieces = rows_in.shape[0]

    def fetch(piece):
        return pltpu.make_async_copy(
            back.at[:, pl.ds(piece * step, step)], rows_in.at[piece], in_sems.at[piece]
        )

    def put(piece):
        return pltpu.make_async_copy(
            rows_out.at[piece], turned.at[pl.ds(piece * step, step)], out_sems.at[piece]
        )

    for piece in range(pieces):
        fetch(piece).start()
    loads = [
        pltpu.make_async_copy(field, narrow.at[number], sems.at[number])
        for number, field in enumerate((innov, rinv, pos))
    ]
    for load in loads:
        load.start()
    for piece in range(pieces):
        fetch(piece).wait()
        for first in range(0, rows_in.shape[3], LANES):
            lanes = slice(first, first + LANES)
            for row in range(0, step, 8):
                block = rows_in[piece, :, row : row + 8, lanes]
                rows_out[piece, row : row + 8, :, lanes] = jnp.swapaxes(block, 0, 1)
        put(piece).start()
    for number, load in enumerate(loads):
        load.wait()
        fields[number] = narrow[number].astype(F32)
    for piece in range(pieces):
        put(piece).wait()


def by_patch_call(background, innov, rinv, pos):
    local, group_patches, width = background.shape
    pieces, step = 4, group_patches // 4
    hbm = pl.BlockSpec(memory_space=pltpu.HBM)
    return pl.pallas_call(
        by_patch_kernel,
        name="by_patch",
        out_shape=[
            jax.ShapeDtypeStruct((group_patches, local, width), BF16),
            pltpu.VMEM((3,) + innov.shape, F32),
        ],
        in_specs=[hbm] * 4,
        out_specs=[hbm, pl.BlockSpec(memory_space=pltpu.VMEM)],
        scratch_shapes=[
            pltpu.VMEM((pieces, local, step, width), BF16),
            pltpu.VMEM((pieces, step, local, width), BF16),
            pltpu.VMEM((3,) + innov.shape, BF16),
            pltpu.SemaphoreType.DMA((pieces,)),
            pltpu.SemaphoreType.DMA((pieces,)),
            pltpu.SemaphoreType.DMA((3,)),
        ],
        compiler_params=pltpu.CompilerParams(vmem_limit_bytes=MOST_VMEM),
        cost_estimate=pl.CostEstimate(
            flops=0, bytes_accessed=4 * background.size, transcendentals=0
        ),
    )(in_hbm(background), in_hbm(innov), in_hbm(rinv), in_hbm(pos))


def edge_kernel(
    given_counts, obs, fields, down, up, counts, count_sem, rows_buf, sems, lhs, acc, accv
):
    patches, _, members = obs.shape
    start_rows([(0, patches - 1, 0)], given_counts, counts, count_sem, obs, rows_buf, sems)
    acc[...] = jnp.zeros_like(acc)
    accv[...] = jnp.zeros_like(accv)
    add_rows(
        0,
        patches - 1,
        0,
        lambda which: (2.0 * which.astype(F32) - 1.0,),
        lambda which: which,
        counts,
        obs,
        fields,
        (rows_buf, sems, lhs, acc, accv),
    )
    row = lax.broadcasted_iota(jnp.int32, (2 * VROWS, members), 0)
    for side, send in enumerate((down, up)):
        send[:members, :] = acc[side * members : (side + 1) * members, :].astype(BF16)
        total = accv[side * VROWS : side * VROWS + 1] + accv[side * VROWS + 1 : side * VROWS + 2]
        high = total.astype(BF16).astype(F32)
        tail = jnp.where(row == 0, high, jnp.where(row == 1, total - high, 0.0))
        send[members:, :] = tail.astype(BF16)


def inner_kernel(
    given_counts, obs, fields, transform, gram, gram_v, counts, count_sem, rows_buf, sems, lhs, acc,
    accv, y_dev, z_dev, p_dev, s_dev
):
    patches, slots, members = obs.shape
    base = 2 * (slots // rows_buf.shape[1])
    pairs = [(1, 1, 0), (0, patches - 1, base)]
    start_rows(pairs, given_counts, counts, count_sem, obs, rows_buf, sems)
    acc[...] = jnp.zeros_like(acc)
    accv[...] = jnp.zeros_like(accv)
    bufs = (rows_buf, sems, lhs, acc, accv)
    add_rows(1, 1, 0, lambda which: OFFSETS, lambda which: which, counts, obs, fields, bufs)
    add_rows(
        0,
        patches - 1,
        base,
        lambda which: (0.0 - which.astype(F32), 1.0 - which.astype(F32)),
        lambda which: which * (patches - 2),
        counts,
        obs,
        fields,
        bufs,
    )
    grams, vecs = [], []
    for t in range(1, patches - 1):
        grams.append(acc[t * members : (t + 1) * members, :])
        vecs.append(accv[t * VROWS : t * VROWS + 1, :] + accv[t * VROWS + 1 : t * VROWS + 2, :])
    for side, t in enumerate((0, patches - 1)):
        gram[side] = acc[t * members : (t + 1) * members, :]
        gram_v[side] = accv[t * VROWS : (t + 1) * VROWS, :]
    root_into(transform, grams, vecs, y_dev, z_dev, p_dev, s_dev)


def gram_call(kernel, name, outs, span, targets, chunks, scratch, flops, counts, obs, fields):
    patches, slots, members = obs.shape
    hbm, vmem = (pl.BlockSpec(memory_space=space) for space in (pltpu.HBM, pltpu.VMEM))
    return pl.pallas_call(
        kernel,
        name=name,
        out_shape=outs,
        in_specs=[hbm, hbm, vmem],
        out_specs=[vmem] * len(outs),
        scratch_shapes=[
            pltpu.SMEM((patches,), jnp.int32),
            pltpu.SemaphoreType.DMA,
            pltpu.VMEM((chunks, CHUNK, members), BF16),
            pltpu.SemaphoreType.DMA((chunks,)),
            pltpu.VMEM((span * members + 4 * VROWS, CHUNK), BF16),
            pltpu.VMEM((targets * members, members), F32),
            pltpu.VMEM((targets * VROWS, members), F32),
        ]
        + scratch,
        compiler_params=pltpu.CompilerParams(vmem_limit_bytes=MOST_VMEM),
        cost_estimate=pl.CostEstimate(
            flops=flops, bytes_accessed=2 * slots * members * 2, transcendentals=6 * slots
        ),
    )(in_hbm(counts), in_hbm(obs), fields)


def scalar_steps():
    return (2.25, -2.4375, 1.6875, -0.5625, 0.0625)


def root_into(transform, grams, vecs, y_dev, z_dev, p_dev, s_dev, between=lambda: None):
    patches = len(grams)
    members = grams[0].shape[1]
    row = lax.broadcasted_iota(jnp.int32, (members, members), 0)
    col = lax.broadcasted_iota(jnp.int32, (members, members), 1)
    diagonal = row == col

    def times(a, a_s, b, b_s):
        product = jnp.dot(a.astype(BF16), b.astype(BF16), preferred_element_type=F32)
        return product + a_s * b + b_s * a

    totals = []
    for t, here in enumerate(grams):
        trace = jnp.sum(jnp.where(diagonal, here, 0.0)) + members * (members - 1.0)
        scale = 1.0 / trace
        y_dev[t] = here * scale + jnp.where(diagonal, (members - 1.0) * scale - 1.0 / members, 0.0)
        totals.append(trace)
    a0, a1, a2, a3, a4 = scalar_steps()
    y_s, z_s = 1.0 / members, 1.0
    for pair in range(NS_STEPS // 2):
        first, final = pair == 0, pair == NS_STEPS // 2 - 1
        p_s = y_s * z_s
        p2_s = p_s * p_s
        h_s = a2 + a3 * p_s + a4 * p2_s
        q_s = p2_s * h_s + a0 + a1 * p_s
        for t in range(patches):
            p_dev[t] = y_dev[t] if first else times(z_dev[t], z_s, y_dev[t], y_s)
        between()
        for t in range(patches):
            s_dev[t] = times(p_dev[t], p_s, p_dev[t], p_s)
        between()
        for t in range(patches):
            p, p2 = p_dev[t], s_dev[t]
            s_dev[t] = times(p2, p2_s, a3 * p + a4 * p2, h_s) + a1 * p
        for t in range(patches):
            q = s_dev[t]
            if not final:
                y_dev[t] = times(y_dev[t], y_s, q, q_s)
            z_dev[t] = q if first else times(z_dev[t], z_s, q, q_s)
        y_s, z_s = y_s * q_s, z_s * q_s
    for t in range(patches):
        z = z_dev[t] + jnp.where(diagonal, z_s, 0.0)
        once = jnp.sum(z * vecs[t], axis=1, keepdims=True)
        twice = jnp.sum(z * once, axis=0, keepdims=True)
        scale = lax.rsqrt(jnp.full((1, members), totals[t], F32) / (members - 1.0))
        transform[t] = (z * scale + twice / totals[t]).astype(BF16)


def apply_to(transform, t, state, out, lanes):
    shares, _, local, _ = state.shape
    wide = state[:, t, :, lanes].astype(F32).reshape(shares * local, LANES)
    center = jnp.sum(wide, axis=0, keepdims=True) * (1.0 / (shares * local))
    spread = (wide - center).astype(BF16)
    result = jnp.dot(transform, spread, preferred_element_type=F32) + center
    out[:, t, :, lanes] = result.astype(BF16).reshape(shares, local, LANES)


def outer_kernel(
    inner, gram, gram_v, from_before, from_after, state, out, transform, y_dev, z_dev, p_dev, s_dev
):
    members = gram.shape[1]
    patches, width = state.shape[1], state.shape[3]
    grams, vecs = [], []
    for t, side in enumerate((from_before, from_after)):
        tail = side[members:, :].astype(F32)
        grams.append(gram[t] + side[:members, :].astype(F32))
        vecs.append(gram_v[t, 0:1, :] + gram_v[t, 1:2, :] + tail[0:1, :] + tail[1:2, :])
    columns = [slice(first, first + LANES) for first in range(0, width, LANES)]
    fill = [(t, lanes) for t in range(1, patches - 1) for lanes in columns]

    def between():
        if fill:
            t, lanes = fill.pop(0)
            apply_to(inner[t - 1], t, state, out, lanes)

    root_into(transform, grams, vecs, y_dev, z_dev, p_dev, s_dev, between)
    while fill:
        between()
    for lanes in columns:
        for side, t in enumerate((0, patches - 1)):
            apply_to(transform[side], t, state, out, lanes)


def outer_call(inner, gram, gram_v, from_before, from_after, state):
    patches, members, _ = gram.shape
    dev = pltpu.VMEM((patches, members, members), F32)
    return pl.pallas_call(
        outer_kernel,
        name="outer",
        out_shape=jax.ShapeDtypeStruct(state.shape, BF16),
        scratch_shapes=[pltpu.VMEM((patches, members, members), BF16)] + [dev] * 4,
        compiler_params=pltpu.CompilerParams(vmem_limit_bytes=40 << 20),
        cost_estimate=pl.CostEstimate(
            flops=17 * patches * 2 * members**3 + 2 * members * state.size,
            bytes_accessed=4 * state.size,
            transcendentals=0,
        ),
    )(inner, gram, gram_v, from_before, from_after, state)


def on_device(background, obs_pert, obs_innov, obs_rinv, obs_pos, obs_count):
    patches, slots, members = obs_pert.shape
    local, group_patches, width = background.shape
    shares = members // local
    pieces = slots // CHUNK
    matmul = 2 * slots * members * members
    by_patch, fields = by_patch_call(background, obs_innov, obs_rinv, obs_pos)
    given = (obs_count, obs_pert, fields)
    state = lax.all_to_all(by_patch, "mem", split_axis=0, concat_axis=0, tiled=True)
    state = state.reshape(shares, patches, local, width)
    to_before, to_after = gram_call(
        edge_kernel,
        "edge",
        [pltpu.VMEM((members + 2 * VROWS, members), BF16)] * 2,
        1,
        2,
        2 * pieces,
        [],
        2 * matmul,
        *given,
    )
    size = lax.axis_size(RING)
    up = [(i, (i + 1) % size) for i in range(size)]
    down = [(j, i) for i, j in up]
    from_after = lax.ppermute(to_before, RING, down)
    from_before = lax.ppermute(to_after, RING, up)
    inner, gram, gram_v = gram_call(
        inner_kernel,
        "inner",
        [
            pltpu.VMEM((patches - 2, members, members), BF16),
            pltpu.VMEM((2, members, members), F32),
            pltpu.VMEM((2, VROWS, members), F32),
        ],
        3,
        patches,
        4 * pieces,
        [pltpu.VMEM((patches - 2, members, members), F32)] * 4,
        10 * matmul,
        *given,
    )
    result = outer_call(inner, gram, gram_v, from_before, from_after, state)
    result = result.reshape(group_patches, local, width)
    result = lax.all_to_all(result, "mem", split_axis=0, concat_axis=0, tiled=True)
    return jnp.swapaxes(result, 0, 1)


def solution(mesh):
    return jax.shard_map(
        on_device,
        mesh=mesh,
        in_specs=(
            P("mem", "grp", None),
            P(("grp", "mem"), None, None),
            P(("grp", "mem"), None),
            P(("grp", "mem"), None),
            P(("grp", "mem"), None),
            P(("grp", "mem")),
        ),
        out_specs=P("mem", "grp", None),
        check_vma=False,
    )
```

```python
import jax
import jax.numpy as jnp
from jax import lax
from jax.experimental import pallas as pl
from jax.experimental.pallas import tpu as pltpu
from jax.sharding import PartitionSpec as P

NS_STEPS = 8
LOC_SCALE = 0.8
CHUNK = 1024
OFFSETS = (-1, 0, 1)
RING = ("grp", "mem")
VROWS = 8
LANES = 128
MOST_VMEM = 40 << 20
F32 = jnp.float32
BF16 = jnp.bfloat16


def in_hbm(array):
    return pltpu.with_memory_space_constraint(array, pltpu.HBM)


def locality(position, inv_var, offset):
    distance = position - 0.5 - offset
    return inv_var * jnp.exp(-distance * distance / (2.0 * LOC_SCALE * LOC_SCALE))


def chunk_products(place, patch, start, offsets, slot, counts, fields, rows_buf, lhs, acc, accv):
    depth, members = rows_buf.shape[1:]
    span = len(offsets)
    live = start + lax.broadcasted_iota(jnp.int32, (1, depth), 1) < counts[patch]
    lanes = pl.ds(pl.multiple_of(start, depth), depth)
    position = fields[2, pl.ds(patch, 1), lanes]
    inv_var = jnp.where(live, fields[1, pl.ds(patch, 1), lanes], 0.0)
    departure = fields[0, pl.ds(patch, 1), lanes]
    turned = rows_buf[place].T.astype(F32)
    row = lax.broadcasted_iota(jnp.int32, (4 * VROWS, depth), 0)
    vec_rows = jnp.zeros((4 * VROWS, depth), F32)
    for number, offset in enumerate(offsets):
        weight = locality(position, inv_var, offset)
        lhs[number * members : (number + 1) * members, :] = (turned * weight).astype(BF16)
        moved = weight * departure
        high = moved.astype(BF16).astype(F32)
        vec_rows = jnp.where(row == number * VROWS, high, vec_rows)
        vec_rows = jnp.where(row == number * VROWS + 1, moved - high, vec_rows)
    lhs[span * members : span * members + 4 * VROWS, :] = vec_rows.astype(BF16)
    product = jnp.dot(
        lhs[: span * members + 4 * VROWS, :], rows_buf[place], preferred_element_type=F32
    )
    first = pl.ds(pl.multiple_of(slot * members, members), span * members)
    acc[first, :] += product[: span * members]
    first_v = pl.ds(pl.multiple_of(slot * VROWS, VROWS), span * VROWS)
    accv[first_v, :] += product[span * members : span * members + span * VROWS]


def start_rows(pairs, given_counts, counts, count_sem, obs, rows_buf, sems):
    depth = rows_buf.shape[1]
    per_patch = obs.shape[1] // depth
    order = []
    for first, step, base in pairs:
        for place in range(2 * per_patch):
            patch, start = first + place // per_patch * step, place % per_patch * depth
            order.append((patch, start, base + place))

    def begin(patch, start, place):
        pltpu.make_async_copy(
            obs.at[patch, pl.ds(start, depth)], rows_buf.at[place], sems.at[place]
        ).start()

    fetch = pltpu.make_async_copy(given_counts, counts, count_sem)
    fetch.start()
    for patch, start, place in order:
        if start == 0:
            begin(patch, start, place)
    fetch.wait()
    for patch, start, place in order:
        if start > 0:
            pl.when(start < counts[patch])(lambda a=(patch, start, place): begin(*a))


def add_rows(first, step, base, offsets_of, slot_of, counts, obs, fields, bufs):
    rows_buf, sems, lhs, acc, accv = bufs
    depth = rows_buf.shape[1]
    per_patch = obs.shape[1] // depth

    def body(place, carry):
        which = place // per_patch
        patch, start = first + which * step, place % per_patch * depth

        @pl.when(start < counts[patch])
        def _():
            rows = pl.ds(pl.multiple_of(start, depth), depth)
            pltpu.make_async_copy(
                obs.at[patch, rows], rows_buf.at[base + place], sems.at[base + place]
            ).wait()
            chunk_products(
                base + place,
                patch,
                start,
                offsets_of(which),
                slot_of(which),
                counts,
                fields,
                rows_buf,
                lhs,
                acc,
                accv,
            )

        return carry

    lax.fori_loop(0, 2 * per_patch, body, 0)


def by_patch_kernel(
    back, innov, rinv, pos, turned, fields, rows_in, rows_out, narrow, in_sems, out_sems, sems
):
    step = rows_in.shape[2]
    pieces = rows_in.shape[0]

    def fetch(piece):
        return pltpu.make_async_copy(
            back.at[:, pl.ds(piece * step, step)], rows_in.at[piece], in_sems.at[piece]
        )

    def put(piece):
        return pltpu.make_async_copy(
            rows_out.at[piece], turned.at[pl.ds(piece * step, step)], out_sems.at[piece]
        )

    for piece in range(pieces):
        fetch(piece).start()
    loads = [
        pltpu.make_async_copy(field, narrow.at[number], sems.at[number])
        for number, field in enumerate((innov, rinv, pos))
    ]
    for load in loads:
        load.start()
    for piece in range(pieces):
        fetch(piece).wait()
        for first in range(0, rows_in.shape[3], LANES):
            lanes = slice(first, first + LANES)
            for row in range(0, step, 8):
                block = rows_in[piece, :, row : row + 8, lanes]
                rows_out[piece, row : row + 8, :, lanes] = jnp.swapaxes(block, 0, 1)
        put(piece).start()
    for number, load in enumerate(loads):
        load.wait()
        fields[number] = narrow[number].astype(F32)
    for piece in range(pieces):
        put(piece).wait()


def by_patch_call(background, innov, rinv, pos):
    local, group_patches, width = background.shape
    pieces, step = 8, group_patches // 8
    hbm = pl.BlockSpec(memory_space=pltpu.HBM)
    return pl.pallas_call(
        by_patch_kernel,
        name="by_patch",
        out_shape=[
            jax.ShapeDtypeStruct((group_patches, local, width), BF16),
            pltpu.VMEM((3,) + innov.shape, F32),
        ],
        in_specs=[hbm] * 4,
        out_specs=[hbm, pl.BlockSpec(memory_space=pltpu.VMEM)],
        scratch_shapes=[
            pltpu.VMEM((pieces, local, step, width), BF16),
            pltpu.VMEM((pieces, step, local, width), BF16),
            pltpu.VMEM((3,) + innov.shape, BF16),
            pltpu.SemaphoreType.DMA((pieces,)),
            pltpu.SemaphoreType.DMA((pieces,)),
            pltpu.SemaphoreType.DMA((3,)),
        ],
        compiler_params=pltpu.CompilerParams(vmem_limit_bytes=MOST_VMEM),
        cost_estimate=pl.CostEstimate(
            flops=0, bytes_accessed=4 * background.size, transcendentals=0
        ),
    )(in_hbm(background), in_hbm(innov), in_hbm(rinv), in_hbm(pos))


def edge_kernel(
    given_counts, obs, fields, near, far, counts, count_sem, rows_buf, sems, lhs, acc, accv
):
    patches, _, members = obs.shape
    start_rows([(0, patches - 1, 0)], given_counts, counts, count_sem, obs, rows_buf, sems)
    acc[...] = jnp.zeros_like(acc)
    accv[...] = jnp.zeros_like(accv)
    add_rows(
        0,
        patches - 1,
        0,
        lambda which: (2.0 * which.astype(F32) - 1.0,),
        lambda which: which,
        counts,
        obs,
        fields,
        (rows_buf, sems, lhs, acc, accv),
    )
    odd = lax.rem(lax.axis_index(RING[1]), 2)
    for side, send in ((1 - odd, near), (odd, far)):
        sums = accv[pl.ds(pl.multiple_of(side * VROWS, VROWS), VROWS), :]
        pack(acc.at[pl.ds(pl.multiple_of(side * members, members), members)], sums, send)


def half_masks(half):
    row = lax.broadcasted_iota(jnp.int32, (half, half), 0)
    col = lax.broadcasted_iota(jnp.int32, (half, half), 1)
    return row, col


def pack(gram, sums, send):
    members = gram.shape[1]
    half = members // 2
    row, col = half_masks(half)
    low = gram[half:, half:]
    send[:half, :half] = jnp.where(col >= row, gram[:half, :half], low).astype(BF16)
    send[:half, half:] = gram[:half, half:].astype(BF16)
    diagonal = jnp.sum(jnp.where(row == col, low, 0.0), axis=0, keepdims=True)
    total = sums[0:1] + sums[1:2]
    high = total.astype(BF16).astype(F32)
    place = lax.broadcasted_iota(jnp.int32, (2 * VROWS, members), 0)
    twice = jnp.concatenate([diagonal, diagonal], axis=1)
    tail = jnp.where(place == 0, high, jnp.where(place == 1, total - high, twice))
    send[half:, :] = tail.astype(BF16)


def unpacked(given):
    half = given.shape[1] // 2
    row, col = half_masks(half)
    shared = given[:half, :half].astype(F32)
    side = given[:half, half:].astype(F32)
    tail = given[half:, :].astype(F32)
    mirrored = shared.T
    top = jnp.where(col >= row, shared, mirrored)
    low = jnp.where(col < row, shared, mirrored)
    low = jnp.where(col == row, tail[2:3, :half], low)
    gram = jnp.concatenate(
        [jnp.concatenate([top, side], axis=1), jnp.concatenate([side.T, low], axis=1)], axis=0
    )
    return gram, tail[0:1, :] + tail[1:2, :]


def inner_kernel(
    given_counts, obs, fields, transform, gram, gram_v, counts, count_sem, rows_buf, sems, lhs, acc,
    accv, y_dev, z_dev, p_dev, s_dev
):
    patches, slots, members = obs.shape
    base = 2 * (slots // rows_buf.shape[1])
    pairs = [(1, 1, 0), (0, patches - 1, base)]
    start_rows(pairs, given_counts, counts, count_sem, obs, rows_buf, sems)
    acc[...] = jnp.zeros_like(acc)
    accv[...] = jnp.zeros_like(accv)
    bufs = (rows_buf, sems, lhs, acc, accv)
    add_rows(1, 1, 0, lambda which: OFFSETS, lambda which: which, counts, obs, fields, bufs)
    add_rows(
        0,
        patches - 1,
        base,
        lambda which: (0.0 - which.astype(F32), 1.0 - which.astype(F32)),
        lambda which: which * (patches - 2),
        counts,
        obs,
        fields,
        bufs,
    )
    grams, vecs = [], []
    for t in range(1, patches - 1):
        grams.append(acc[t * members : (t + 1) * members, :])
        vecs.append(accv[t * VROWS : t * VROWS + 1, :] + accv[t * VROWS + 1 : t * VROWS + 2, :])
    for side, t in enumerate((0, patches - 1)):
        gram[side] = acc[t * members : (t + 1) * members, :]
        gram_v[side] = accv[t * VROWS : (t + 1) * VROWS, :]
    root_into(transform, grams, vecs, y_dev, z_dev, p_dev, s_dev)


def gram_call(kernel, name, outs, span, targets, chunks, scratch, flops, counts, obs, fields):
    patches, slots, members = obs.shape
    hbm, vmem = (pl.BlockSpec(memory_space=space) for space in (pltpu.HBM, pltpu.VMEM))
    return pl.pallas_call(
        kernel,
        name=name,
        out_shape=outs,
        in_specs=[hbm, hbm, vmem],
        out_specs=[vmem] * len(outs),
        scratch_shapes=[
            pltpu.SMEM((patches,), jnp.int32),
            pltpu.SemaphoreType.DMA,
            pltpu.VMEM((chunks, CHUNK, members), BF16),
            pltpu.SemaphoreType.DMA((chunks,)),
            pltpu.VMEM((span * members + 4 * VROWS, CHUNK), BF16),
            pltpu.VMEM((targets * members, members), F32),
            pltpu.VMEM((targets * VROWS, members), F32),
        ]
        + scratch,
        compiler_params=pltpu.CompilerParams(vmem_limit_bytes=MOST_VMEM),
        cost_estimate=pl.CostEstimate(
            flops=flops, bytes_accessed=2 * slots * members * 2, transcendentals=6 * slots
        ),
    )(in_hbm(counts), in_hbm(obs), fields)


def scalar_steps():
    return (2.25, -2.4375, 1.6875, -0.5625, 0.0625)


def root_into(transform, grams, vecs, y_dev, z_dev, p_dev, s_dev, between=lambda: None):
    patches = len(grams)
    members = grams[0].shape[1]
    row = lax.broadcasted_iota(jnp.int32, (members, members), 0)
    col = lax.broadcasted_iota(jnp.int32, (members, members), 1)
    diagonal = row == col

    def matmul(a, b):
        return jnp.dot(a.astype(BF16), b.astype(BF16), preferred_element_type=F32)

    def times(a, b):
        return matmul(a, b) + (a + b)

    totals = []
    for t, here in enumerate(grams):
        trace = jnp.sum(jnp.where(diagonal, here, 0.0)) + members * (members - 1.0)
        scale = members / trace
        y_dev[t] = here * scale + jnp.where(diagonal, (members - 1.0) * scale - 1.0, 0.0)
        totals.append(trace)
    a0, a1, a2, a3, a4 = scalar_steps()
    y_s, z_s = 1.0 / members, 1.0
    for pair in range(NS_STEPS // 2):
        first, final = pair == 0, pair == NS_STEPS // 2 - 1
        p_s = y_s * z_s
        p2_s = p_s * p_s
        h_s = a2 + a3 * p_s + a4 * p2_s
        q_s = p2_s * h_s + a0 + a1 * p_s
        h_p, h_p2 = a3 * p_s / h_s, a4 * p2_s / h_s
        q_h, q_p = p2_s * h_s / q_s, a1 * p_s / q_s
        for t in range(patches):
            p_dev[t] = y_dev[t] if first else times(z_dev[t], y_dev[t])
        between()
        for t in range(patches):
            p = p_dev[t]
            s_dev[t] = matmul(p, p) + (p + p)
        between()
        for t in range(patches):
            p, p2 = p_dev[t], s_dev[t]
            product = matmul(p2, h_p * p + h_p2 * p2)
            s_dev[t] = q_h * product + ((q_h * h_p + q_p) * p + (q_h + q_h * h_p2) * p2)
        for t in range(patches):
            q = s_dev[t]
            if not final:
                y_dev[t] = times(y_dev[t], q)
            z_dev[t] = q if first else times(z_dev[t], q)
        y_s, z_s = y_s * q_s, z_s * q_s
    for t in range(patches):
        z = z_dev[t] + jnp.where(diagonal, 1.0, 0.0)
        once = jnp.sum(z * vecs[t], axis=1, keepdims=True)
        twice = jnp.sum(z * once, axis=0, keepdims=True)
        total = jnp.full((1, members), totals[t], F32)
        scale = z_s * lax.rsqrt(total / (members - 1.0))
        transform[t] = (z * scale + twice * (z_s * z_s) / total).astype(BF16)


def apply_to(transform, t, state, out, lanes):
    shares, _, local, _ = state.shape
    wide = state[:, t, :, lanes].astype(F32).reshape(shares * local, LANES)
    center = jnp.sum(wide, axis=0, keepdims=True) * (1.0 / (shares * local))
    spread = (wide - center).astype(BF16)
    result = jnp.dot(transform, spread, preferred_element_type=F32) + center
    out[:, t, :, lanes] = result.astype(BF16).reshape(shares, local, LANES)


def columns_of(state):
    return [slice(first, first + LANES) for first in range(0, state.shape[3], LANES)]


def outer_kernel(
    inner, gram, gram_v, near, far, state, out, transform, y_dev, z_dev, p_dev, s_dev
):
    members = gram.shape[1]
    patches = state.shape[1]
    odd = lax.rem(lax.axis_index(RING[1]), 2)
    sides = (1 - odd, odd)
    grams, vecs = [], []
    for side, given in zip(sides, (near, far)):
        other, other_v = unpacked(given)
        grams.append(gram[side] + other)
        own = gram_v[side]
        vecs.append(own[0:1, :] + own[1:2, :] + other_v)
    fill = [(t, lanes) for t in range(1, patches - 1) for lanes in columns_of(state)]

    def between():
        if fill:
            t, lanes = fill.pop(0)
            apply_to(inner[t - 1], t, state, out, lanes)

    root_into(transform, grams, vecs, y_dev, z_dev, p_dev, s_dev, between)
    while fill:
        between()
    for lanes in columns_of(state):
        for number, side in enumerate(sides):
            apply_to(transform[number], side * (patches - 1), state, out, lanes)


def outer_call(inner, gram, gram_v, near, far, state):
    patches, members, _ = gram.shape
    dev = pltpu.VMEM((patches, members, members), F32)
    return pl.pallas_call(
        outer_kernel,
        name="outer",
        out_shape=pltpu.VMEM(state.shape, BF16),
        scratch_shapes=[pltpu.VMEM((patches, members, members), BF16)] + [dev] * 4,
        compiler_params=pltpu.CompilerParams(vmem_limit_bytes=MOST_VMEM),
        cost_estimate=pl.CostEstimate(
            flops=17 * patches * 2 * members**3 + members * state.size,
            bytes_accessed=2 * state.size,
            transcendentals=0,
        ),
    )(inner, gram, gram_v, near, far, state)


def by_member_kernel(given, out, rows_out, sems):
    pieces, _, step, width = rows_out.shape

    def put(piece):
        return pltpu.make_async_copy(
            rows_out.at[piece], out.at[:, pl.ds(piece * step, step)], sems.at[piece]
        )

    for piece in range(pieces):
        for first in range(0, width, LANES):
            lanes = slice(first, first + LANES)
            for row in range(0, step, 8):
                place = piece * step + row
                block = given[place : place + 8, :, lanes]
                rows_out[piece, :, row : row + 8, lanes] = jnp.swapaxes(block, 0, 1)
        put(piece).start()
    for piece in range(pieces):
        put(piece).wait()


def by_member_call(given):
    group_patches, local, width = given.shape
    pieces, step = 8, group_patches // 8
    return pl.pallas_call(
        by_member_kernel,
        name="by_member",
        out_shape=jax.ShapeDtypeStruct((local, group_patches, width), BF16),
        in_specs=[pl.BlockSpec(memory_space=pltpu.VMEM)],
        out_specs=pl.BlockSpec(memory_space=pltpu.HBM),
        scratch_shapes=[
            pltpu.VMEM((pieces, local, step, width), BF16),
            pltpu.SemaphoreType.DMA((pieces,)),
        ],
        compiler_params=pltpu.CompilerParams(vmem_limit_bytes=MOST_VMEM),
        cost_estimate=pl.CostEstimate(flops=0, bytes_accessed=4 * given.size, transcendentals=0),
    )(given)


def on_device(background, obs_pert, obs_innov, obs_rinv, obs_pos, obs_count):
    patches, slots, members = obs_pert.shape
    local, group_patches, width = background.shape
    shares = members // local
    pieces = slots // CHUNK
    matmul = 2 * slots * members * members
    by_patch, fields = by_patch_call(background, obs_innov, obs_rinv, obs_pos)
    given = (obs_count, obs_pert, fields)
    state = lax.all_to_all(by_patch, "mem", split_axis=0, concat_axis=0, tiled=True)
    state = state.reshape(shares, patches, local, width)
    to_near, to_far = gram_call(
        edge_kernel,
        "edge",
        [pltpu.VMEM((members // 2 + 2 * VROWS, members), BF16)] * 2,
        1,
        2,
        2 * pieces,
        [],
        2 * matmul,
        *given,
    )
    size = lax.axis_size(RING)
    from_near = lax.ppermute(to_near, RING, [(i, i ^ 1) for i in range(size)])
    from_far = lax.ppermute(
        to_far, RING, [(i, (i + 1 if i % 2 else i - 1) % size) for i in range(size)]
    )
    inner, gram, gram_v = gram_call(
        inner_kernel,
        "inner",
        [
            pltpu.VMEM((patches - 2, members, members), BF16),
            pltpu.VMEM((2, members, members), F32),
            pltpu.VMEM((2, VROWS, members), F32),
        ],
        3,
        patches,
        4 * pieces,
        [pltpu.VMEM((patches - 2, members, members), F32)] * 4,
        10 * matmul,
        *given,
    )
    result = outer_call(inner, gram, gram_v, from_near, from_far, state)
    result = result.reshape(group_patches, local, width)
    result = lax.all_to_all(result, "mem", split_axis=0, concat_axis=0, tiled=True)
    return by_member_call(result)


def solution(mesh):
    return jax.shard_map(
        on_device,
        mesh=mesh,
        in_specs=(
            P("mem", "grp", None),
            P(("grp", "mem"), None, None),
            P(("grp", "mem"), None),
            P(("grp", "mem"), None),
            P(("grp", "mem"), None),
            P(("grp", "mem")),
        ),
        out_specs=P("mem", "grp", None),
        check_vma=False,
    )
```

```python
import functools
import jax
import jax.numpy as jnp
from jax import lax
from jax.experimental import pallas as pl
from jax.experimental.pallas import tpu as pltpu
from jax.sharding import PartitionSpec as P

NS_STEPS = 8
LOC_SCALE = 0.8
CHUNK = 1024
OFFSETS = (-1, 0, 1)
RING = ("grp", "mem")
VROWS = 8
LANES = 128
WIDE = 256
MOST_VMEM = 40 << 20
F32 = jnp.float32
BF16 = jnp.bfloat16


def in_hbm(array):
    return pltpu.with_memory_space_constraint(array, pltpu.HBM)


def locality(position, inv_var, offset):
    distance = position - 0.5 - offset
    return inv_var * jnp.exp(-distance * distance / (2.0 * LOC_SCALE * LOC_SCALE))


def chunk_products(place, patch, start, offsets, slot, counts, fields, rows_buf, lhs, acc, accv):
    depth, members = rows_buf.shape[1:]
    span = len(offsets)
    live = start + lax.broadcasted_iota(jnp.int32, (1, depth), 1) < counts[patch]
    lanes = pl.ds(pl.multiple_of(start, depth), depth)
    position = fields[2, pl.ds(patch, 1), lanes]
    inv_var = jnp.where(live, fields[1, pl.ds(patch, 1), lanes], 0.0)
    departure = fields[0, pl.ds(patch, 1), lanes]
    turned = rows_buf[place].T.astype(F32)
    row = lax.broadcasted_iota(jnp.int32, (4 * VROWS, depth), 0)
    vec_rows = jnp.zeros((4 * VROWS, depth), F32)
    for number, offset in enumerate(offsets):
        weight = locality(position, inv_var, offset)
        lhs[number * members : (number + 1) * members, :] = (turned * weight).astype(BF16)
        moved = weight * departure
        high = moved.astype(BF16).astype(F32)
        vec_rows = jnp.where(row == number * VROWS, high, vec_rows)
        vec_rows = jnp.where(row == number * VROWS + 1, moved - high, vec_rows)
    lhs[span * members : span * members + 4 * VROWS, :] = vec_rows.astype(BF16)
    product = jnp.dot(
        lhs[: span * members + 4 * VROWS, :], rows_buf[place], preferred_element_type=F32
    )
    first = pl.ds(pl.multiple_of(slot * members, members), span * members)
    acc[first, :] += product[: span * members]
    first_v = pl.ds(pl.multiple_of(slot * VROWS, VROWS), span * VROWS)
    accv[first_v, :] += product[span * members : span * members + span * VROWS]


def start_rows(pairs, given_counts, counts, count_sem, obs, rows_buf, sems):
    depth = rows_buf.shape[1]
    per_patch = obs.shape[1] // depth
    order = []
    for first, step, base in pairs:
        for place in range(2 * per_patch):
            patch, start = first + place // per_patch * step, place % per_patch * depth
            order.append((patch, start, base + place))

    def begin(patch, start, place):
        pltpu.make_async_copy(
            obs.at[patch, pl.ds(start, depth)], rows_buf.at[place], sems.at[place]
        ).start()

    fetch = pltpu.make_async_copy(given_counts, counts, count_sem)
    fetch.start()
    for patch, start, place in order:
        if start == 0:
            begin(patch, start, place)
    fetch.wait()
    for patch, start, place in order:
        if start > 0:
            pl.when(start < counts[patch])(lambda a=(patch, start, place): begin(*a))


def add_rows(first, step, base, offsets_of, slot_of, counts, obs, fields, bufs):
    rows_buf, sems, lhs, acc, accv = bufs
    depth = rows_buf.shape[1]
    per_patch = obs.shape[1] // depth

    def body(place, carry):
        which = place // per_patch
        patch, start = first + which * step, place % per_patch * depth

        @pl.when(start < counts[patch])
        def _():
            rows = pl.ds(pl.multiple_of(start, depth), depth)
            pltpu.make_async_copy(
                obs.at[patch, rows], rows_buf.at[base + place], sems.at[base + place]
            ).wait()
            chunk_products(
                base + place,
                patch,
                start,
                offsets_of(which),
                slot_of(which),
                counts,
                fields,
                rows_buf,
                lhs,
                acc,
                accv,
            )

        return carry

    lax.fori_loop(0, 2 * per_patch, body, 0)


def share_place(share, shares):
    flip = lax.rem(lax.axis_index(RING[0]), 2)
    return share + flip * (shares - 1 - 2 * share)


def by_patch_kernel(
    back, innov, rinv, pos, turned, fields, rows_in, rows_out, narrow, in_sems, out_sems, sems
):
    step = rows_in.shape[2]
    pieces = rows_in.shape[0]
    group_patches, patches = back.shape[1], innov.shape[0]

    def fetch(piece):
        return pltpu.make_async_copy(
            back.at[:, pl.ds(piece * step, step)], rows_in.at[piece], in_sems.at[piece]
        )

    shares, share = group_patches // patches, patches

    def put(piece):
        copies = []
        for part in range(step // share):
            place = share_place(piece * (step // share) + part, shares)
            copies.append(
                pltpu.make_async_copy(
                    rows_out.at[piece, pl.ds(part * share, share)],
                    turned.at[pl.ds(place * share, share)],
                    out_sems.at[piece * (step // share) + part],
                )
            )
        return copies

    for piece in range(pieces):
        fetch(piece).start()
    loads = [
        pltpu.make_async_copy(field, narrow.at[number], sems.at[number])
        for number, field in enumerate((innov, rinv, pos))
    ]
    for load in loads:
        load.start()
    for piece in range(pieces):
        fetch(piece).wait()
        for first in range(0, rows_in.shape[3], LANES):
            lanes = slice(first, first + LANES)
            for row in range(0, step, 8):
                block = rows_in[piece, :, row : row + 8, lanes]
                rows_out[piece, row : row + 8, :, lanes] = jnp.swapaxes(block, 0, 1)
        for copy in put(piece):
            copy.start()
    for number, load in enumerate(loads):
        load.wait()
        fields[number] = narrow[number].astype(F32)
    for piece in range(pieces):
        for copy in put(piece):
            copy.wait()


def by_patch_call(background, innov, rinv, pos):
    local, group_patches, width = background.shape
    pieces, step = 8, group_patches // 8
    hbm = pl.BlockSpec(memory_space=pltpu.HBM)
    return pl.pallas_call(
        by_patch_kernel,
        name="by_patch",
        out_shape=[
            jax.ShapeDtypeStruct((group_patches, local, width), BF16),
            pltpu.VMEM((3,) + innov.shape, F32),
        ],
        in_specs=[hbm] * 4,
        out_specs=[hbm, pl.BlockSpec(memory_space=pltpu.VMEM)],
        scratch_shapes=[
            pltpu.VMEM((pieces, local, step, width), BF16),
            pltpu.VMEM((pieces, step, local, width), BF16),
            pltpu.VMEM((3,) + innov.shape, BF16),
            pltpu.SemaphoreType.DMA((pieces,)),
            pltpu.SemaphoreType.DMA((group_patches // innov.shape[0],)),
            pltpu.SemaphoreType.DMA((3,)),
        ],
        compiler_params=pltpu.CompilerParams(vmem_limit_bytes=MOST_VMEM),
        cost_estimate=pl.CostEstimate(
            flops=0, bytes_accessed=4 * background.size, transcendentals=0
        ),
    )(in_hbm(background), in_hbm(innov), in_hbm(rinv), in_hbm(pos))


def edge_kernel(
    given_counts, obs, fields, near, far, counts, count_sem, rows_buf, sems, lhs, acc, accv
):
    patches, _, members = obs.shape
    start_rows([(0, patches - 1, 0)], given_counts, counts, count_sem, obs, rows_buf, sems)
    acc[...] = jnp.zeros_like(acc)
    accv[...] = jnp.zeros_like(accv)
    add_rows(
        0,
        patches - 1,
        0,
        lambda which: (2.0 * which.astype(F32) - 1.0,),
        lambda which: which,
        counts,
        obs,
        fields,
        (rows_buf, sems, lhs, acc, accv),
    )
    odd = lax.rem(lax.axis_index(RING[1]), 2)
    for side, send in ((1 - odd, near), (odd, far)):
        sums = accv[pl.ds(pl.multiple_of(side * VROWS, VROWS), VROWS), :]
        pack(acc.at[pl.ds(pl.multiple_of(side * members, members), members)], sums, send)


def half_masks(half):
    row = lax.broadcasted_iota(jnp.int32, (half, half), 0)
    col = lax.broadcasted_iota(jnp.int32, (half, half), 1)
    return row, col


def pack(gram, sums, send):
    members = gram.shape[1]
    half = members // 2
    row, col = half_masks(half)
    low = gram[half:, half:]
    send[:half, :half] = jnp.where(col >= row, gram[:half, :half], low).astype(BF16)
    send[:half, half:] = gram[:half, half:].astype(BF16)
    diagonal = jnp.sum(jnp.where(row == col, low, 0.0), axis=0, keepdims=True)
    total = sums[0:1] + sums[1:2]
    high = total.astype(BF16).astype(F32)
    place = lax.broadcasted_iota(jnp.int32, (2 * VROWS, members), 0)
    twice = jnp.concatenate([diagonal, diagonal], axis=1)
    tail = jnp.where(place == 0, high, jnp.where(place == 1, total - high, twice))
    send[half:, :] = tail.astype(BF16)


def unpacked(given):
    half = given.shape[1] // 2
    row, col = half_masks(half)
    shared = given[:half, :half].astype(F32)
    side = given[:half, half:].astype(F32)
    tail = given[half:, :].astype(F32)
    mirrored = shared.T
    top = jnp.where(col >= row, shared, mirrored)
    low = jnp.where(col < row, shared, mirrored)
    low = jnp.where(col == row, tail[2:3, :half], low)
    gram = jnp.concatenate(
        [jnp.concatenate([top, side], axis=1), jnp.concatenate([side.T, low], axis=1)], axis=0
    )
    return gram, tail[0:1, :] + tail[1:2, :]


def inner_kernel(
    given_counts, obs, fields, transform, gram, gram_v, counts, count_sem, rows_buf, sems, lhs, acc,
    accv, y_dev, z_dev, p_dev, s_dev
):
    patches, slots, members = obs.shape
    base = 2 * (slots // rows_buf.shape[1])
    pairs = [(1, 1, 0), (0, patches - 1, base)]
    start_rows(pairs, given_counts, counts, count_sem, obs, rows_buf, sems)
    acc[...] = jnp.zeros_like(acc)
    accv[...] = jnp.zeros_like(accv)
    bufs = (rows_buf, sems, lhs, acc, accv)
    add_rows(1, 1, 0, lambda which: OFFSETS, lambda which: which, counts, obs, fields, bufs)
    add_rows(
        0,
        patches - 1,
        base,
        lambda which: (0.0 - which.astype(F32), 1.0 - which.astype(F32)),
        lambda which: which * (patches - 2),
        counts,
        obs,
        fields,
        bufs,
    )
    grams, vecs = [], []
    for t in range(1, patches - 1):
        grams.append(acc[t * members : (t + 1) * members, :])
        vecs.append(accv[t * VROWS : t * VROWS + 1, :] + accv[t * VROWS + 1 : t * VROWS + 2, :])
    for side, t in enumerate((0, patches - 1)):
        gram[side] = acc[t * members : (t + 1) * members, :]
        gram_v[side] = accv[t * VROWS : (t + 1) * VROWS, :]
    root_into(transform, grams, vecs, y_dev, z_dev, p_dev, s_dev)


def gram_call(kernel, name, outs, span, targets, chunks, scratch, flops, counts, obs, fields):
    patches, slots, members = obs.shape
    hbm, vmem = (pl.BlockSpec(memory_space=space) for space in (pltpu.HBM, pltpu.VMEM))
    return pl.pallas_call(
        kernel,
        name=name,
        out_shape=outs,
        in_specs=[hbm, hbm, vmem],
        out_specs=[vmem] * len(outs),
        scratch_shapes=[
            pltpu.SMEM((patches,), jnp.int32),
            pltpu.SemaphoreType.DMA,
            pltpu.VMEM((chunks, CHUNK, members), BF16),
            pltpu.SemaphoreType.DMA((chunks,)),
            pltpu.VMEM((span * members + 4 * VROWS, CHUNK), BF16),
            pltpu.VMEM((targets * members, members), F32),
            pltpu.VMEM((targets * VROWS, members), F32),
        ]
        + scratch,
        compiler_params=pltpu.CompilerParams(vmem_limit_bytes=MOST_VMEM),
        cost_estimate=pl.CostEstimate(
            flops=flops, bytes_accessed=2 * slots * members * 2, transcendentals=6 * slots
        ),
    )(in_hbm(counts), in_hbm(obs), fields)


def scalar_steps():
    return (2.25, -2.4375, 1.6875, -0.5625, 0.0625)


def root_into(transform, grams, vecs, y_dev, z_dev, p_dev, s_dev, between=lambda: None):
    patches = len(grams)
    members = grams[0].shape[1]
    row = lax.broadcasted_iota(jnp.int32, (members, members), 0)
    col = lax.broadcasted_iota(jnp.int32, (members, members), 1)
    diagonal = row == col

    def matmul(a, b):
        return jnp.dot(a.astype(BF16), b.astype(BF16), preferred_element_type=F32)

    def times(a, b):
        return matmul(a, b) + (a + b)

    totals = []
    for t, here in enumerate(grams):
        trace = jnp.sum(jnp.where(diagonal, here, 0.0)) + members * (members - 1.0)
        scale = members / trace
        y_dev[t] = here * scale + jnp.where(diagonal, (members - 1.0) * scale - 1.0, 0.0)
        totals.append(trace)
    a0, a1, a2, a3, a4 = scalar_steps()
    y_s, z_s = 1.0 / members, 1.0
    for pair in range(NS_STEPS // 2):
        first, final = pair == 0, pair == NS_STEPS // 2 - 1
        p_s = y_s * z_s
        p2_s = p_s * p_s
        h_s = a2 + a3 * p_s + a4 * p2_s
        q_s = p2_s * h_s + a0 + a1 * p_s
        h_p, h_p2 = a3 * p_s / h_s, a4 * p2_s / h_s
        q_h, q_p = p2_s * h_s / q_s, a1 * p_s / q_s
        for t in range(patches):
            p_dev[t] = y_dev[t] if first else times(z_dev[t], y_dev[t])
        between()
        for t in range(patches):
            p = p_dev[t]
            s_dev[t] = matmul(p, p) + (p + p)
        between()
        for t in range(patches):
            p, p2 = p_dev[t], s_dev[t]
            product = matmul(p2, h_p * p + h_p2 * p2)
            s_dev[t] = q_h * product + ((q_h * h_p + q_p) * p + (q_h + q_h * h_p2) * p2)
        for t in range(patches):
            q = s_dev[t]
            if first or final:
                if not final:
                    y_dev[t] = times(y_dev[t], q)
                z_dev[t] = q if first else times(z_dev[t], q)
            else:
                both = matmul(jnp.concatenate([y_dev[t], z_dev[t]], axis=0), q)
                y_dev[t] = both[:members] + (y_dev[t] + q)
                z_dev[t] = both[members:] + (z_dev[t] + q)
        y_s, z_s = y_s * q_s, z_s * q_s
    for t in range(patches):
        z = z_dev[t] + jnp.where(diagonal, 1.0, 0.0)
        once = jnp.sum(z * vecs[t], axis=1, keepdims=True)
        twice = jnp.sum(z * once, axis=0, keepdims=True)
        total = jnp.full((1, members), totals[t], F32)
        scale = z_s * lax.rsqrt(total / (members - 1.0))
        transform[t] = (z * scale + twice * (z_s * z_s) / total).astype(BF16)


def apply_to(transform, t, state, out, lanes):
    shares, _, local, _ = state.shape
    parts = [state[share_place(share, shares), t, :, lanes] for share in range(shares)]
    wide = jnp.concatenate(parts, axis=0).astype(F32)
    center = jnp.sum(wide, axis=0, keepdims=True) * (1.0 / (shares * local))
    spread = (wide - center).astype(BF16)
    result = jnp.dot(transform, spread, preferred_element_type=F32) + center
    result = result.astype(BF16)
    for share in range(shares):
        out[share_place(share, shares), t, :, lanes] = result[share * local : (share + 1) * local]


def columns_of(state):
    return [slice(first, first + WIDE) for first in range(0, state.shape[3], WIDE)]


def outer_kernel(
    inner, gram, gram_v, near, far, state, out, transform, y_dev, z_dev, p_dev, s_dev
):
    members = gram.shape[1]
    patches = state.shape[1]
    odd = lax.rem(lax.axis_index(RING[1]), 2)
    sides = (1 - odd, odd)
    grams, vecs = [], []
    for side, given in zip(sides, (near, far)):
        other, other_v = unpacked(given)
        grams.append(gram[side] + other)
        own = gram_v[side]
        vecs.append(own[0:1, :] + own[1:2, :] + other_v)
    fill = [(t, lanes) for t in range(1, patches - 1) for lanes in columns_of(state)]

    def between():
        if fill:
            t, lanes = fill.pop(0)
            apply_to(inner[t - 1], t, state, out, lanes)

    root_into(transform, grams, vecs, y_dev, z_dev, p_dev, s_dev, between)
    while fill:
        between()
    for lanes in columns_of(state):
        for number, side in enumerate(sides):
            apply_to(transform[number], side * (patches - 1), state, out, lanes)


def outer_call(inner, gram, gram_v, near, far, state):
    patches, members, _ = gram.shape
    dev = pltpu.VMEM((patches, members, members), F32)
    return pl.pallas_call(
        outer_kernel,
        name="outer",
        out_shape=pltpu.VMEM(state.shape, BF16),
        scratch_shapes=[pltpu.VMEM((patches, members, members), BF16)] + [dev] * 4,
        compiler_params=pltpu.CompilerParams(vmem_limit_bytes=MOST_VMEM),
        cost_estimate=pl.CostEstimate(
            flops=17 * patches * 2 * members**3 + members * state.size,
            bytes_accessed=2 * state.size,
            transcendentals=0,
        ),
    )(inner, gram, gram_v, near, far, state)


def by_member_kernel(shares, given, out, rows_out, sems):
    pieces, _, step, width = rows_out.shape
    share = given.shape[0] // shares

    def put(piece):
        return pltpu.make_async_copy(
            rows_out.at[piece], out.at[:, pl.ds(piece * step, step)], sems.at[piece]
        )

    for piece in range(pieces):
        for first in range(0, width, LANES):
            lanes = slice(first, first + LANES)
            for row in range(0, step, 8):
                first_share = (piece * step + row) // share
                block = jnp.concatenate(
                    [
                        given[
                            pl.ds(share_place(first_share + part, shares) * share, share), :, lanes
                        ]
                        for part in range(8 // share)
                    ],
                    axis=0,
                )
                rows_out[piece, :, row : row + 8, lanes] = jnp.swapaxes(block, 0, 1)
        put(piece).start()
    for piece in range(pieces):
        put(piece).wait()


def by_member_call(shares, given):
    group_patches, local, width = given.shape
    pieces, step = 8, group_patches // 8
    return pl.pallas_call(
        functools.partial(by_member_kernel, shares),
        name="by_member",
        out_shape=jax.ShapeDtypeStruct((local, group_patches, width), BF16),
        in_specs=[pl.BlockSpec(memory_space=pltpu.VMEM)],
        out_specs=pl.BlockSpec(memory_space=pltpu.HBM),
        scratch_shapes=[
            pltpu.VMEM((pieces, local, step, width), BF16),
            pltpu.SemaphoreType.DMA((pieces,)),
        ],
        compiler_params=pltpu.CompilerParams(vmem_limit_bytes=MOST_VMEM),
        cost_estimate=pl.CostEstimate(flops=0, bytes_accessed=4 * given.size, transcendentals=0),
    )(given)


def on_device(background, obs_pert, obs_innov, obs_rinv, obs_pos, obs_count):
    patches, slots, members = obs_pert.shape
    local, group_patches, width = background.shape
    shares = members // local
    pieces = slots // CHUNK
    matmul = 2 * slots * members * members
    by_patch, fields = by_patch_call(background, obs_innov, obs_rinv, obs_pos)
    given = (obs_count, obs_pert, fields)
    orders = [
        [group * shares + (shares - 1 - place if group % 2 else place) for place in range(shares)]
        for group in range(lax.axis_size(RING[0]))
    ]
    state = lax.all_to_all(
        by_patch, RING, split_axis=0, concat_axis=0, axis_index_groups=orders, tiled=True
    )
    state = state.reshape(shares, patches, local, width)
    to_near, to_far = gram_call(
        edge_kernel,
        "edge",
        [pltpu.VMEM((members // 2 + 2 * VROWS, members), BF16)] * 2,
        1,
        2,
        2 * pieces,
        [],
        2 * matmul,
        *given,
    )
    size = lax.axis_size(RING)
    from_near = lax.ppermute(to_near, RING, [(i, i ^ 1) for i in range(size)])
    from_far = lax.ppermute(
        to_far, RING, [(i, (i + 1 if i % 2 else i - 1) % size) for i in range(size)]
    )
    inner, gram, gram_v = gram_call(
        inner_kernel,
        "inner",
        [
            pltpu.VMEM((patches - 2, members, members), BF16),
            pltpu.VMEM((2, members, members), F32),
            pltpu.VMEM((2, VROWS, members), F32),
        ],
        3,
        patches,
        4 * pieces,
        [pltpu.VMEM((patches - 2, members, members), F32)] * 4,
        10 * matmul,
        *given,
    )
    result = outer_call(inner, gram, gram_v, from_near, from_far, state)
    result = result.reshape(group_patches, local, width)
    result = lax.all_to_all(
        result, RING, split_axis=0, concat_axis=0, axis_index_groups=orders, tiled=True
    )
    return by_member_call(shares, result)


def solution(mesh):
    return jax.shard_map(
        on_device,
        mesh=mesh,
        in_specs=(
            P("mem", "grp", None),
            P(("grp", "mem"), None, None),
            P(("grp", "mem"), None),
            P(("grp", "mem"), None),
            P(("grp", "mem"), None),
            P(("grp", "mem")),
        ),
        out_specs=P("mem", "grp", None),
        check_vma=False,
    )
```

```python
import functools
import math
import jax
import jax.numpy as jnp
from jax import lax
from jax.experimental import pallas as pl
from jax.experimental.pallas import tpu as pltpu
from jax.sharding import PartitionSpec as P

NS_STEPS = 8
LOC_SCALE = 0.8
CHUNK = 1024
OFFSETS = (-1, 0, 1)
RING = ("grp", "mem")
VROWS = 8
LANES = 128
WIDE = 256
MOST_VMEM = 40 << 20
F32 = jnp.float32
BF16 = jnp.bfloat16


def in_hbm(array):
    return pltpu.with_memory_space_constraint(array, pltpu.HBM)


def locality(position, inv_var, offset):
    distance = position - 0.5 - offset
    return inv_var * jnp.exp(-distance * distance / (2.0 * LOC_SCALE * LOC_SCALE))


def chunk_products(place, patch, start, offsets, slot, counts, fields, rows_buf, lhs, acc, accv):
    depth, members = rows_buf.shape[1:]
    span = len(offsets)
    live = start + lax.broadcasted_iota(jnp.int32, (1, depth), 1) < counts[patch]
    lanes = pl.ds(pl.multiple_of(start, depth), depth)
    position = fields[2, pl.ds(patch, 1), lanes]
    inv_var = jnp.where(live, fields[1, pl.ds(patch, 1), lanes], 0.0)
    departure = fields[0, pl.ds(patch, 1), lanes]
    turned = rows_buf[place].T.astype(F32)
    row = lax.broadcasted_iota(jnp.int32, (4 * VROWS, depth), 0)
    vec_rows = jnp.zeros((4 * VROWS, depth), F32)
    for number, offset in enumerate(offsets):
        weight = locality(position, inv_var, offset)
        lhs[number * members : (number + 1) * members, :] = (turned * weight).astype(BF16)
        moved = weight * departure
        high = moved.astype(BF16).astype(F32)
        vec_rows = jnp.where(row == number * VROWS, high, vec_rows)
        vec_rows = jnp.where(row == number * VROWS + 1, moved - high, vec_rows)
    lhs[span * members : span * members + 4 * VROWS, :] = vec_rows.astype(BF16)
    product = jnp.dot(
        lhs[: span * members + 4 * VROWS, :], rows_buf[place], preferred_element_type=F32
    )
    first = pl.ds(pl.multiple_of(slot * members, members), span * members)
    acc[first, :] += product[: span * members]
    first_v = pl.ds(pl.multiple_of(slot * VROWS, VROWS), span * VROWS)
    accv[first_v, :] += product[span * members : span * members + span * VROWS]


def start_rows(pairs, given_counts, counts, count_sem, obs, rows_buf, sems):
    depth = rows_buf.shape[1]
    per_patch = obs.shape[1] // depth
    order = []
    for first, step, base in pairs:
        for place in range(2 * per_patch):
            patch, start = first + place // per_patch * step, place % per_patch * depth
            order.append((patch, start, base + place))

    def begin(patch, start, place):
        pltpu.make_async_copy(
            obs.at[patch, pl.ds(start, depth)], rows_buf.at[place], sems.at[place]
        ).start()

    fetch = pltpu.make_async_copy(given_counts, counts, count_sem)
    fetch.start()
    for patch, start, place in order:
        if start == 0:
            begin(patch, start, place)
    fetch.wait()
    for patch, start, place in order:
        if start > 0:
            pl.when(start < counts[patch])(lambda a=(patch, start, place): begin(*a))


def add_rows(first, step, base, offsets_of, slot_of, counts, obs, fields, bufs):
    rows_buf, sems, lhs, acc, accv = bufs
    depth = rows_buf.shape[1]
    per_patch = obs.shape[1] // depth

    def body(place, carry):
        which = place // per_patch
        patch, start = first + which * step, place % per_patch * depth

        @pl.when(start < counts[patch])
        def _():
            rows = pl.ds(pl.multiple_of(start, depth), depth)
            pltpu.make_async_copy(
                obs.at[patch, rows], rows_buf.at[base + place], sems.at[base + place]
            ).wait()
            chunk_products(
                base + place,
                patch,
                start,
                offsets_of(which),
                slot_of(which),
                counts,
                fields,
                rows_buf,
                lhs,
                acc,
                accv,
            )

        return carry

    lax.fori_loop(0, 2 * per_patch, body, 0)


def exchange_orders(shares):
    side = math.isqrt(shares)
    spread = [x + side * ((x + y) % side) for y in range(side) for x in range(side)]
    return spread, spread[::-1]


def share_place(share, shares):
    first, second = (order.index(share) for order in exchange_orders(shares))
    return first + lax.rem(lax.axis_index(RING[0]), 2) * (second - first)


def by_patch_kernel(
    back, innov, rinv, pos, turned, fields, rows_in, rows_out, narrow, in_sems, out_sems, sems
):
    step = rows_in.shape[2]
    pieces = rows_in.shape[0]
    group_patches, patches = back.shape[1], innov.shape[0]

    def fetch(piece):
        return pltpu.make_async_copy(
            back.at[:, pl.ds(piece * step, step)], rows_in.at[piece], in_sems.at[piece]
        )

    shares, share = group_patches // patches, patches

    def put(piece):
        copies = []
        for part in range(step // share):
            place = share_place(piece * (step // share) + part, shares)
            copies.append(
                pltpu.make_async_copy(
                    rows_out.at[piece, pl.ds(part * share, share)],
                    turned.at[pl.ds(place * share, share)],
                    out_sems.at[piece * (step // share) + part],
                )
            )
        return copies

    for piece in range(pieces):
        fetch(piece).start()
    loads = [
        pltpu.make_async_copy(field, narrow.at[number], sems.at[number])
        for number, field in enumerate((innov, rinv, pos))
    ]
    for load in loads:
        load.start()
    for piece in range(pieces):
        fetch(piece).wait()
        for first in range(0, rows_in.shape[3], LANES):
            lanes = slice(first, first + LANES)
            for row in range(0, step, 8):
                block = rows_in[piece, :, row : row + 8, lanes]
                rows_out[piece, row : row + 8, :, lanes] = jnp.swapaxes(block, 0, 1)
        for copy in put(piece):
            copy.start()
    for number, load in enumerate(loads):
        load.wait()
        fields[number] = narrow[number].astype(F32)
    for piece in range(pieces):
        for copy in put(piece):
            copy.wait()


def by_patch_call(background, innov, rinv, pos):
    local, group_patches, width = background.shape
    pieces, step = 8, group_patches // 8
    hbm = pl.BlockSpec(memory_space=pltpu.HBM)
    return pl.pallas_call(
        by_patch_kernel,
        name="by_patch",
        out_shape=[
            jax.ShapeDtypeStruct((group_patches, local, width), BF16),
            pltpu.VMEM((3,) + innov.shape, F32),
        ],
        in_specs=[hbm] * 4,
        out_specs=[hbm, pl.BlockSpec(memory_space=pltpu.VMEM)],
        scratch_shapes=[
            pltpu.VMEM((pieces, local, step, width), BF16),
            pltpu.VMEM((pieces, step, local, width), BF16),
            pltpu.VMEM((3,) + innov.shape, BF16),
            pltpu.SemaphoreType.DMA((pieces,)),
            pltpu.SemaphoreType.DMA((group_patches // innov.shape[0],)),
            pltpu.SemaphoreType.DMA((3,)),
        ],
        compiler_params=pltpu.CompilerParams(vmem_limit_bytes=MOST_VMEM),
        cost_estimate=pl.CostEstimate(
            flops=0, bytes_accessed=4 * background.size, transcendentals=0
        ),
    )(in_hbm(background), in_hbm(innov), in_hbm(rinv), in_hbm(pos))


def edge_kernel(
    given_counts, obs, fields, near, far, counts, count_sem, rows_buf, sems, lhs, acc, accv
):
    patches, _, members = obs.shape
    start_rows([(0, patches - 1, 0)], given_counts, counts, count_sem, obs, rows_buf, sems)
    acc[...] = jnp.zeros_like(acc)
    accv[...] = jnp.zeros_like(accv)
    add_rows(
        0,
        patches - 1,
        0,
        lambda which: (2.0 * which.astype(F32) - 1.0,),
        lambda which: which,
        counts,
        obs,
        fields,
        (rows_buf, sems, lhs, acc, accv),
    )
    odd = lax.rem(lax.axis_index(RING[1]), 2)
    for side, send in ((1 - odd, near), (odd, far)):
        sums = accv[pl.ds(pl.multiple_of(side * VROWS, VROWS), VROWS), :]
        pack(acc.at[pl.ds(pl.multiple_of(side * members, members), members)], sums, send)


def half_masks(half):
    row = lax.broadcasted_iota(jnp.int32, (half, half), 0)
    col = lax.broadcasted_iota(jnp.int32, (half, half), 1)
    return row, col


def pack(gram, sums, send):
    members = gram.shape[1]
    half = members // 2
    row, col = half_masks(half)
    low = gram[half:, half:]
    send[:half, :half] = jnp.where(col >= row, gram[:half, :half], low).astype(BF16)
    send[:half, half:] = gram[:half, half:].astype(BF16)
    diagonal = jnp.sum(jnp.where(row == col, low, 0.0), axis=0, keepdims=True)
    total = sums[0:1] + sums[1:2]
    high = total.astype(BF16).astype(F32)
    place = lax.broadcasted_iota(jnp.int32, (2 * VROWS, members), 0)
    twice = jnp.concatenate([diagonal, diagonal], axis=1)
    tail = jnp.where(place == 0, high, jnp.where(place == 1, total - high, twice))
    send[half:, :] = tail.astype(BF16)


def unpacked(given):
    half = given.shape[1] // 2
    row, col = half_masks(half)
    shared = given[:half, :half].astype(F32)
    side = given[:half, half:].astype(F32)
    tail = given[half:, :].astype(F32)
    mirrored = shared.T
    top = jnp.where(col >= row, shared, mirrored)
    low = jnp.where(col < row, shared, mirrored)
    low = jnp.where(col == row, tail[2:3, :half], low)
    gram = jnp.concatenate(
        [jnp.concatenate([top, side], axis=1), jnp.concatenate([side.T, low], axis=1)], axis=0
    )
    return gram, tail[0:1, :] + tail[1:2, :]


def inner_kernel(
    given_counts, obs, fields, transform, gram, gram_v, counts, count_sem, rows_buf, sems, lhs, acc,
    accv, y_dev, z_dev, p_dev, s_dev
):
    patches, slots, members = obs.shape
    base = 2 * (slots // rows_buf.shape[1])
    pairs = [(1, 1, 0), (0, patches - 1, base)]
    start_rows(pairs, given_counts, counts, count_sem, obs, rows_buf, sems)
    acc[...] = jnp.zeros_like(acc)
    accv[...] = jnp.zeros_like(accv)
    bufs = (rows_buf, sems, lhs, acc, accv)
    add_rows(1, 1, 0, lambda which: OFFSETS, lambda which: which, counts, obs, fields, bufs)
    add_rows(
        0,
        patches - 1,
        base,
        lambda which: (0.0 - which.astype(F32), 1.0 - which.astype(F32)),
        lambda which: which * (patches - 2),
        counts,
        obs,
        fields,
        bufs,
    )
    grams, vecs = [], []
    for t in range(1, patches - 1):
        grams.append(acc[t * members : (t + 1) * members, :])
        vecs.append(accv[t * VROWS : t * VROWS + 1, :] + accv[t * VROWS + 1 : t * VROWS + 2, :])
    for side, t in enumerate((0, patches - 1)):
        gram[side] = acc[t * members : (t + 1) * members, :]
        gram_v[side] = accv[t * VROWS : (t + 1) * VROWS, :]
    root_into(transform, grams, vecs, y_dev, z_dev, p_dev, s_dev)


def gram_call(kernel, name, outs, span, targets, chunks, scratch, flops, counts, obs, fields):
    patches, slots, members = obs.shape
    hbm, vmem = (pl.BlockSpec(memory_space=space) for space in (pltpu.HBM, pltpu.VMEM))
    return pl.pallas_call(
        kernel,
        name=name,
        out_shape=outs,
        in_specs=[hbm, hbm, vmem],
        out_specs=[vmem] * len(outs),
        scratch_shapes=[
            pltpu.SMEM((patches,), jnp.int32),
            pltpu.SemaphoreType.DMA,
            pltpu.VMEM((chunks, CHUNK, members), BF16),
            pltpu.SemaphoreType.DMA((chunks,)),
            pltpu.VMEM((span * members + 4 * VROWS, CHUNK), BF16),
            pltpu.VMEM((targets * members, members), F32),
            pltpu.VMEM((targets * VROWS, members), F32),
        ]
        + scratch,
        compiler_params=pltpu.CompilerParams(vmem_limit_bytes=MOST_VMEM),
        cost_estimate=pl.CostEstimate(
            flops=flops, bytes_accessed=2 * slots * members * 2, transcendentals=6 * slots
        ),
    )(in_hbm(counts), in_hbm(obs), fields)


def scalar_steps():
    return (2.25, -2.4375, 1.6875, -0.5625, 0.0625)


def root_into(transform, grams, vecs, y_dev, z_dev, p_dev, s_dev, between=lambda: None):
    patches = len(grams)
    members = grams[0].shape[1]
    row = lax.broadcasted_iota(jnp.int32, (members, members), 0)
    col = lax.broadcasted_iota(jnp.int32, (members, members), 1)
    diagonal = row == col

    def matmul(a, b):
        return jnp.dot(a.astype(BF16), b.astype(BF16), preferred_element_type=F32)

    def times(a, b):
        return matmul(a, b) + (a + b)

    totals = []
    for t, here in enumerate(grams):
        trace = jnp.sum(jnp.where(diagonal, here, 0.0)) + members * (members - 1.0)
        scale = members / trace
        y_dev[t] = here * scale + jnp.where(diagonal, (members - 1.0) * scale - 1.0, 0.0)
        totals.append(trace)
    a0, a1, a2, a3, a4 = scalar_steps()
    y_s, z_s = 1.0 / members, 1.0
    for pair in range(NS_STEPS // 2):
        first, final = pair == 0, pair == NS_STEPS // 2 - 1
        p_s = y_s * z_s
        p2_s = p_s * p_s
        h_s = a2 + a3 * p_s + a4 * p2_s
        q_s = p2_s * h_s + a0 + a1 * p_s
        h_p, h_p2 = a3 * p_s / h_s, a4 * p2_s / h_s
        q_h, q_p = p2_s * h_s / q_s, a1 * p_s / q_s
        for t in range(patches):
            p_dev[t] = y_dev[t] if first else times(z_dev[t], y_dev[t])
        between()
        for t in range(patches):
            p = p_dev[t]
            s_dev[t] = matmul(p, p) + (p + p)
        between()
        for t in range(patches):
            p, p2 = p_dev[t], s_dev[t]
            product = matmul(p2, h_p * p + h_p2 * p2)
            s_dev[t] = q_h * product + ((q_h * h_p + q_p) * p + (q_h + q_h * h_p2) * p2)
        for t in range(patches):
            q = s_dev[t]
            if first or final:
                if not final:
                    y_dev[t] = times(y_dev[t], q)
                z_dev[t] = q if first else times(z_dev[t], q)
            else:
                both = matmul(jnp.concatenate([y_dev[t], z_dev[t]], axis=0), q)
                y_dev[t] = both[:members] + (y_dev[t] + q)
                z_dev[t] = both[members:] + (z_dev[t] + q)
        y_s, z_s = y_s * q_s, z_s * q_s
    for t in range(patches):
        z = z_dev[t] + jnp.where(diagonal, 1.0, 0.0)
        once = jnp.sum(z * vecs[t], axis=1, keepdims=True)
        twice = jnp.sum(z * once, axis=0, keepdims=True)
        total = jnp.full((1, members), totals[t], F32)
        scale = z_s * lax.rsqrt(total / (members - 1.0))
        transform[t] = (z * scale + twice * (z_s * z_s) / total).astype(BF16)


def apply_to(transform, t, state, out, lanes):
    shares, _, local, _ = state.shape
    parts = [state[share_place(share, shares), t, :, lanes] for share in range(shares)]
    wide = jnp.concatenate(parts, axis=0).astype(F32)
    center = jnp.sum(wide, axis=0, keepdims=True) * (1.0 / (shares * local))
    spread = (wide - center).astype(BF16)
    result = jnp.dot(transform, spread, preferred_element_type=F32) + center
    result = result.astype(BF16)
    for share in range(shares):
        out[share_place(share, shares), t, :, lanes] = result[share * local : (share + 1) * local]


def columns_of(state):
    return [slice(first, first + WIDE) for first in range(0, state.shape[3], WIDE)]


def outer_kernel(
    inner, gram, gram_v, near, far, state, out, transform, y_dev, z_dev, p_dev, s_dev
):
    members = gram.shape[1]
    patches = state.shape[1]
    odd = lax.rem(lax.axis_index(RING[1]), 2)
    sides = (1 - odd, odd)
    grams, vecs = [], []
    for side, given in zip(sides, (near, far)):
        other, other_v = unpacked(given)
        grams.append(gram[side] + other)
        own = gram_v[side]
        vecs.append(own[0:1, :] + own[1:2, :] + other_v)
    fill = [(t, lanes) for t in range(1, patches - 1) for lanes in columns_of(state)]

    def between():
        if fill:
            t, lanes = fill.pop(0)
            apply_to(inner[t - 1], t, state, out, lanes)

    root_into(transform, grams, vecs, y_dev, z_dev, p_dev, s_dev, between)
    while fill:
        between()
    for lanes in columns_of(state):
        for number, side in enumerate(sides):
            apply_to(transform[number], side * (patches - 1), state, out, lanes)


def outer_call(inner, gram, gram_v, near, far, state):
    patches, members, _ = gram.shape
    dev = pltpu.VMEM((patches, members, members), F32)
    return pl.pallas_call(
        outer_kernel,
        name="outer",
        out_shape=pltpu.VMEM(state.shape, BF16),
        scratch_shapes=[pltpu.VMEM((patches, members, members), BF16)] + [dev] * 4,
        compiler_params=pltpu.CompilerParams(vmem_limit_bytes=MOST_VMEM),
        cost_estimate=pl.CostEstimate(
            flops=17 * patches * 2 * members**3 + members * state.size,
            bytes_accessed=2 * state.size,
            transcendentals=0,
        ),
    )(inner, gram, gram_v, near, far, state)


def by_member_kernel(shares, given, out, rows_out, sems):
    pieces, _, step, width = rows_out.shape
    share = given.shape[0] // shares

    def put(piece):
        return pltpu.make_async_copy(
            rows_out.at[piece], out.at[:, pl.ds(piece * step, step)], sems.at[piece]
        )

    for piece in range(pieces):
        for first in range(0, width, LANES):
            lanes = slice(first, first + LANES)
            for row in range(0, step, 8):
                first_share = (piece * step + row) // share
                block = jnp.concatenate(
                    [
                        given[
                            pl.ds(share_place(first_share + part, shares) * share, share), :, lanes
                        ]
                        for part in range(8 // share)
                    ],
                    axis=0,
                )
                rows_out[piece, :, row : row + 8, lanes] = jnp.swapaxes(block, 0, 1)
        put(piece).start()
    for piece in range(pieces):
        put(piece).wait()


def by_member_call(shares, given):
    group_patches, local, width = given.shape
    pieces, step = 8, group_patches // 8
    return pl.pallas_call(
        functools.partial(by_member_kernel, shares),
        name="by_member",
        out_shape=jax.ShapeDtypeStruct((local, group_patches, width), BF16),
        in_specs=[pl.BlockSpec(memory_space=pltpu.VMEM)],
        out_specs=pl.BlockSpec(memory_space=pltpu.HBM),
        scratch_shapes=[
            pltpu.VMEM((pieces, local, step, width), BF16),
            pltpu.SemaphoreType.DMA((pieces,)),
        ],
        compiler_params=pltpu.CompilerParams(vmem_limit_bytes=MOST_VMEM),
        cost_estimate=pl.CostEstimate(flops=0, bytes_accessed=4 * given.size, transcendentals=0),
    )(given)


def on_device(background, obs_pert, obs_innov, obs_rinv, obs_pos, obs_count):
    patches, slots, members = obs_pert.shape
    local, group_patches, width = background.shape
    shares = members // local
    pieces = slots // CHUNK
    matmul = 2 * slots * members * members
    by_patch, fields = by_patch_call(background, obs_innov, obs_rinv, obs_pos)
    given = (obs_count, obs_pert, fields)
    by_core = exchange_orders(shares)
    orders = [
        [group * shares + device for device in by_core[group % 2]]
        for group in range(lax.axis_size(RING[0]))
    ]
    state = lax.all_to_all(
        by_patch, RING, split_axis=0, concat_axis=0, axis_index_groups=orders, tiled=True
    )
    state = state.reshape(shares, patches, local, width)
    to_near, to_far = gram_call(
        edge_kernel,
        "edge",
        [pltpu.VMEM((members // 2 + 2 * VROWS, members), BF16)] * 2,
        1,
        2,
        2 * pieces,
        [],
        2 * matmul,
        *given,
    )
    size = lax.axis_size(RING)
    from_near = lax.ppermute(to_near, RING, [(i, i ^ 1) for i in range(size)])
    from_far = lax.ppermute(
        to_far, RING, [(i, (i + 1 if i % 2 else i - 1) % size) for i in range(size)]
    )
    inner, gram, gram_v = gram_call(
        inner_kernel,
        "inner",
        [
            pltpu.VMEM((patches - 2, members, members), BF16),
            pltpu.VMEM((2, members, members), F32),
            pltpu.VMEM((2, VROWS, members), F32),
        ],
        3,
        patches,
        4 * pieces,
        [pltpu.VMEM((patches - 2, members, members), F32)] * 4,
        10 * matmul,
        *given,
    )
    result = outer_call(inner, gram, gram_v, from_near, from_far, state)
    result = result.reshape(group_patches, local, width)
    result = lax.all_to_all(
        result, RING, split_axis=0, concat_axis=0, axis_index_groups=orders, tiled=True
    )
    return by_member_call(shares, result)


def solution(mesh):
    return jax.shard_map(
        on_device,
        mesh=mesh,
        in_specs=(
            P("mem", "grp", None),
            P(("grp", "mem"), None, None),
            P(("grp", "mem"), None),
            P(("grp", "mem"), None),
            P(("grp", "mem"), None),
            P(("grp", "mem")),
        ),
        out_specs=P("mem", "grp", None),
        check_vma=False,
    )
```
